512 devices in a mesh: dp: 128 (over y, z, core), mp: 4 (over x).
Axes of the slice: x: 4, y: 8, z: 8, core: 2. Of those that a mesh axis runs over, the one named last changes fastest.
Arguments:
- frames: bfloat16 [32768, 1024], P('dp'), may hold values from -24 to 24
- proj_in: bfloat16 [1024, 2, 1024], P(None, None, 'mp'), may hold values from -0.1875 to 0.1875
- depthwise: float32 [31, 1024], P(None, 'mp'), may hold values from -1 to 1
- bn_gain: float32 [1024], P('mp'), may hold values from 0.5 to 1.5
- bn_shift: float32 [1024], P('mp'), may hold values from -3 to 3
- proj_out: bfloat16 [1024, 1024], P(None, 'mp'), may hold values from -0.1875 to 0.1875
- grad_out: bfloat16 [32768, 1024], P('dp'), may hold values from -24 to 24
- counts: int32 [128], replicated, may hold values from 1 to 2, as said below
- lengths: int32 [128, 2], P('dp'), may hold values from 1 to 255, as said below
Outputs:
- frame_grad: bfloat16 [32768, 1024], P('dp', 'mp')
- in_grad: float32 [1024, 2, 1024], P('dp', None, 'mp')
- out_grad: float32 [1024, 1024], P('dp', 'mp')
- depth_grad: float32 [31, 1024], P(None, 'mp')
- gain_grad: float32 [1024], P('mp')
- shift_grad: float32 [1024], P('mp')
The draws below stay inside these ranges and needn't reach their ends.
Inputs may be any that keep to these rules, and one draw needn't show every extreme that they name: `counts`: some device holds 2 live blocks. lengths[d] sums to 128 * counts[d]; on some device with 2 live blocks one utterance holds all frames but one for each other utterance.
All inputs are finite; a program needn't handle non-finite values.
Results may differ from the reference program's by a relative error of at most 0.0095.
Values may be sent and summed in bfloat16 or wider, within the bound.
No kernel may reach another device: no remote copies, remote signals or barrier semaphores. Data moves between devices by JAX's collectives and lax.ppermute only.
A program may use at most 64 MiB of HBM per device.

```python
import jax
import jax.numpy as jnp
from jax import lax

D = 1024
K = 31
BLOCK = 128
BLK_DEV = 2
UTT_DEV = 2
FRAMES = 32768
N_DP = 128
N_MP = 4


def block_plan(key):
    base_key = jax.random.fold_in(key, 7)
    count_key, pick_key, split_key = jax.random.split(base_key, 3)
    counts = jax.random.randint(count_key, (N_DP,), 1, BLK_DEV + 1, dtype=jnp.int32)
    chosen = jax.random.randint(pick_key, (), 0, N_DP, dtype=jnp.int32)
    is_chosen = jnp.arange(N_DP, dtype=jnp.int32) == chosen
    counts = jnp.where(is_chosen, BLK_DEV, counts).astype(jnp.int32)
    weights = jax.random.randint(split_key, (N_DP, UTT_DEV), 1, 1001, dtype=jnp.int32)
    spare_frames = counts * BLOCK - UTT_DEV
    shares = 1 + spare_frames[:, None] * weights // jnp.sum(weights, axis=1, keepdims=True)
    leading = shares[:, :-1]
    final_len = counts * BLOCK - jnp.sum(leading, axis=1)
    lengths = jnp.concatenate([leading, final_len[:, None]], axis=1).astype(jnp.int32)
    utt_pos = jnp.arange(UTT_DEV, dtype=jnp.int32)
    extreme = jnp.where(utt_pos == UTT_DEV - 1, BLK_DEV * BLOCK - UTT_DEV + 1, 1).astype(jnp.int32)
    lengths = jnp.where(is_chosen[:, None], extreme[None, :], lengths).astype(jnp.int32)
    return (counts, lengths)


def draw_counts(key, part):
    return block_plan(key)[0]


def draw_lengths(key, part):
    return block_plan(key)[1]


def draw_frames(key, part):
    base_key = jax.random.fold_in(key, 11)
    noise_key, scale_key, pick_key, pair_key = jax.random.split(base_key, 4)
    rows_dev = BLK_DEV * BLOCK
    dev_of_row = (jnp.arange(FRAMES, dtype=jnp.int32) // rows_dev).astype(jnp.int32)
    ramp = jnp.arange(N_DP, dtype=jnp.float32) / float(max(N_DP - 1, 1))
    chosen = jax.random.randint(pick_key, (), 0, N_DP, dtype=jnp.int32)
    is_chosen = jnp.arange(N_DP, dtype=jnp.int32) == chosen
    pairing = jax.random.permutation(pair_key, N_DP).astype(jnp.int32)
    col_block = (jnp.arange(D, dtype=jnp.int32) // (D // N_DP)).astype(jnp.int32)
    spike = jnp.where(col_block[None, :] == pairing[dev_of_row][:, None], 3.0, 1.0).astype(jnp.float32)
    base_vals = jax.random.normal(noise_key, (FRAMES, D), jnp.float32)
    jitter = jnp.exp(jax.random.uniform(scale_key, (N_DP,), jnp.float32, 0.0, 1.1939225))
    dev_scale = (1.0 + 2.0 * ramp) * jitter
    dev_scale = jnp.where(is_chosen, 12.0, dev_scale)
    values = base_vals * dev_scale[dev_of_row][:, None] * spike
    return jnp.clip(values, -24.0, 24.0).astype(jnp.bfloat16)


def spiked(array, own_key, source, target, shards_of, factor):
    owner, partner = [(jnp.arange(array.shape[dim]) // (array.shape[dim] // shards_of)).reshape([-1 if axis == dim else 1 for axis in range(array.ndim)]) for dim in (source, target)]
    chosen = jax.random.permutation(own_key, shards_of)[partner]
    strong = (owner == chosen) | (owner == (partner + shards_of // 2) % shards_of)
    return jnp.where(strong, factor * array, array)


def steps_of(stream_key, dims, cuts, low, high):
    factor_of, own = 1.0, jax.random.fold_in(stream_key, 6)
    for dim, parts in cuts:
        steps = jnp.exp(jax.random.uniform(jax.random.fold_in(own, dim), (parts,), jnp.float32, low / len(cuts), high / len(cuts)))
        factor_of = factor_of * jnp.repeat(steps, dims[dim] // parts).reshape([-1 if axis == dim else 1 for axis in range(len(dims))])
    return factor_of


def bell_draw(rng, extent, spread, most, pieces=(), held_as=jnp.bfloat16):
    array = spread * jax.random.normal(rng, extent, jnp.float32)
    if pieces:
        array = array * steps_of(rng, extent, pieces, -0.22, 0.18)
    return jnp.clip(array, -most, most).astype(held_as)


def bell_draw_with(own_key, dims, deviation, limit, shards, heavy, kind=jnp.bfloat16):
    array = deviation * jax.random.normal(own_key, dims, jnp.float32)
    if shards:
        array = array * steps_of(own_key, dims, shards, -0.22, 0.18)
    return jnp.clip(spiked(array, jax.random.fold_in(own_key, 3), *heavy), -limit, limit).astype(kind)


def setup_inputs(seed: int = 0) -> dict:
    splits = jax.random.split(jax.random.key(seed), 10)
    return {
        "frames": draw_frames(jax.random.fold_in(splits[9], 71), 0),
        "proj_in": bell_draw(splits[1], (D, 2, D), D ** -0.5, 0.1875, ((2, 4),)),
        "depthwise": bell_draw(splits[2], (K, D), K ** -0.5, 1.0, ((1, 4),), jnp.float32),
        "bn_gain": jnp.clip(0.5 + 1.0 * jax.random.uniform(splits[3], (D,), jnp.float32) ** steps_of(splits[3], (D,), ((0, 4),), -0.2, 0.2), 0.5, 1.5),
        "bn_shift": bell_draw(splits[4], (D,), 0.5, 3.0, ((0, 4),), jnp.float32),
        "proj_out": bell_draw(splits[5], (D, D), D ** -0.5, 0.1875, ((1, 4),)),
        "grad_out": bell_draw_with(splits[6], (FRAMES, D), 1.0, 24.0, ((0, 128),), (0, 1, 128, 5.5)),
        "counts": draw_counts(jax.random.fold_in(splits[9], 71), 0),
        "lengths": draw_lengths(jax.random.fold_in(splits[9], 71), 0),
    }


def time_shift(values, offset, fill_value):
    if offset > 0:
        pad_part = jnp.full((offset,) + values.shape[1:], fill_value, values.dtype)
        return jnp.concatenate([values[offset:], pad_part], axis=0)
    if offset < 0:
        pad_part = jnp.full((-offset,) + values.shape[1:], fill_value, values.dtype)
        return jnp.concatenate([pad_part, values[:offset]], axis=0)
    return values

def layout(counts, lengths):
    slots_dev = BLK_DEV * BLOCK
    position = jnp.arange(slots_dev, dtype=jnp.int32)
    utt_ends = jnp.cumsum(lengths, axis=1).astype(jnp.int32)
    seg_index = lax.optimization_barrier(jnp.sum((position[None, :, None] >= utt_ends[:, None, :]).astype(jnp.int32), axis=2)).astype(jnp.int32)
    live_mask = (position[None, :] < (counts * BLOCK).astype(jnp.int32)[:, None]).astype(jnp.float32)
    owner_id = (jnp.arange(N_DP, dtype=jnp.int32)[:, None] * (UTT_DEV + 1) + seg_index).astype(jnp.int32)
    return (owner_id.reshape(-1), live_mask.reshape(-1)[:, None])

def reference(frames, proj_in, depthwise, bn_gain, bn_shift, proj_out, grad_out, counts, lengths):
    owner_id, live_col = layout(counts, lengths)
    frame_total = (jnp.sum(counts) * BLOCK).astype(jnp.float32)
    radius = K // 2
    pre_act = jnp.dot(frames, proj_in.reshape(D, 2 * D), preferred_element_type=jnp.float32).reshape(-1, 2, D)
    value_half = pre_act[:, 0]
    gate_sig = jax.nn.sigmoid(pre_act[:, 1])
    glu_out = (value_half * gate_sig * live_col).astype(jnp.bfloat16)
    glu_float = lax.optimization_barrier(glu_out).astype(jnp.float32)
    conv_out = jnp.zeros(glu_float.shape, jnp.float32)
    for tap_index in range(K):
        offset = tap_index - radius
        same_utt = (time_shift(owner_id, offset, -1) == owner_id).astype(jnp.float32)[:, None] * live_col
        conv_out = conv_out + depthwise[tap_index] * (time_shift(glu_float, offset, 0.0) * same_utt)
    mean_val = lax.optimization_barrier(jnp.sum(conv_out, axis=0)) / frame_total
    square_mean = lax.optimization_barrier(jnp.sum(conv_out * conv_out, axis=0)) / frame_total
    inv_std = lax.rsqrt(square_mean - mean_val * mean_val + 1e-05)
    normed = (conv_out - mean_val) * inv_std
    scaled = normed * bn_gain + bn_shift
    sig_scaled = jax.nn.sigmoid(scaled)
    hidden = (scaled * sig_scaled * live_col).astype(jnp.bfloat16)
    grad_hidden = jnp.dot(grad_out, proj_out, preferred_element_type=jnp.float32) * live_col
    grad_scaled = grad_hidden * sig_scaled * (1.0 + scaled * (1.0 - sig_scaled))
    shift_grad = lax.optimization_barrier(jnp.sum(grad_scaled, axis=0))
    gain_grad = lax.optimization_barrier(jnp.sum(grad_scaled * normed, axis=0))
    grad_conv = live_col * bn_gain * inv_std * (grad_scaled - shift_grad / frame_total - normed * gain_grad / frame_total)
    depth_rows = []
    grad_glu = jnp.zeros(glu_float.shape, jnp.float32)
    for tap_index in range(K):
        offset = tap_index - radius
        same_utt = (time_shift(owner_id, offset, -1) == owner_id).astype(jnp.float32)[:, None] * live_col
        depth_rows.append(lax.optimization_barrier(jnp.sum(grad_conv * (time_shift(glu_float, offset, 0.0) * same_utt), axis=0)))
        back_same = (time_shift(owner_id, -offset, -1) == owner_id).astype(jnp.float32)[:, None] * live_col
        grad_glu = grad_glu + depthwise[tap_index] * time_shift(grad_conv, -offset, 0.0) * back_same
    depth_grad = jnp.stack(depth_rows)
    grad_value = grad_glu * gate_sig
    grad_gate = grad_glu * value_half * gate_sig * (1.0 - gate_sig)
    grad_pre = jnp.stack([grad_value, grad_gate], axis=1).astype(jnp.bfloat16)
    group_width = D // N_MP
    grad_groups = grad_pre.reshape(-1, 2, N_MP, group_width)
    proj_groups = proj_in.reshape(D, 2, N_MP, group_width)
    frame_sum = jnp.zeros((grad_pre.shape[0], D), jnp.float32)
    for group_index in range(N_MP):
        left_part = grad_groups[:, :, group_index].reshape(-1, 2 * group_width)
        right_part = proj_groups[:, :, group_index].reshape(D, 2 * group_width)
        partial_value = lax.dot_general(left_part, right_part, (((1,), (1,)), ((), ())), preferred_element_type=jnp.float32)
        frame_sum = frame_sum + lax.optimization_barrier(partial_value.astype(jnp.bfloat16)).astype(jnp.float32)
    frame_grad = frame_sum.astype(jnp.bfloat16)
    in_grad = lax.dot_general(frames, grad_pre.reshape(-1, 2 * D), (((0,), (0,)), ((), ())), preferred_element_type=jnp.float32).reshape(D, 2, D)
    out_grad = lax.dot_general(grad_out, hidden, (((0,), (0,)), ((), ())), preferred_element_type=jnp.float32)
    return (frame_grad, in_grad, out_grad, depth_grad, gain_grad, shift_grad)
```

```python
import jax
import jax.numpy as jnp
from jax import lax
from jax.sharding import Mesh, PartitionSpec as P

BLOCK = 128
DP = ("y", "z", "core")


def time_shift(values, offset, fill_value):
    if offset > 0:
        pad_part = jnp.full((offset,) + values.shape[1:], fill_value, values.dtype)
        return jnp.concatenate([values[offset:], pad_part], axis=0)
    if offset < 0:
        pad_part = jnp.full((-offset,) + values.shape[1:], fill_value, values.dtype)
        return jnp.concatenate([pad_part, values[:offset]], axis=0)
    return values


def tap_term(glu_float, owner_id, live_col, offset):
    same_utt = (time_shift(owner_id, offset, -1) == owner_id).astype(jnp.float32)[
        :, None
    ] * live_col
    return time_shift(glu_float, offset, 0.0) * same_utt


def small_sum(x):
    x = lax.psum(x, "core")
    peers = lax.axis_size("y") * lax.axis_size("z")
    every = jnp.broadcast_to(x[None], (peers,) + x.shape)
    return jnp.sum(lax.all_to_all(every, ("y", "z"), 0, 0), axis=0)


def scatter_sum(partial):
    peers = lax.axis_size("y") * lax.axis_size("z")
    rows = partial.shape[0] // (2 * peers)
    parts = partial.reshape(peers, 2, rows, partial.shape[1])
    core = lax.axis_index("core")
    keep = lax.dynamic_index_in_dim(parts, core, 1, keepdims=False)
    send = lax.dynamic_index_in_dim(parts, 1 - core, 1, keepdims=False).astype(jnp.bfloat16)
    got = lax.ppermute(send, "core", [(0, 1), (1, 0)])
    both = (keep + got.astype(jnp.float32)).astype(jnp.bfloat16)
    every = lax.all_to_all(both, ("y", "z"), 0, 0)
    return jnp.sum(every.astype(jnp.float32), axis=0)


def shards(frames, proj_in, depthwise, bn_gain, bn_shift, proj_out, grad_out, counts, lengths):
    frames_dev = frames.shape[0]
    model_width = frames.shape[1]
    channels = proj_in.shape[2]
    tap_count = depthwise.shape[0]
    radius = tap_count // 2
    rows_dev = model_width // lax.axis_size(DP)
    groups = lax.axis_size("mp")
    position = jnp.arange(frames_dev, dtype=jnp.int32)
    utt_ends = jnp.cumsum(lengths[0])
    owner_id = jnp.sum((position[:, None] >= utt_ends[None, :]).astype(jnp.int32), axis=1)
    my_count = counts[lax.axis_index(DP)]
    live_col = (position < my_count * BLOCK).astype(jnp.float32)[:, None]
    frame_total = (jnp.sum(counts) * BLOCK).astype(jnp.float32)
    proj_flat = proj_in.reshape(model_width, 2 * channels)
    pre_act = jnp.dot(frames, proj_flat, preferred_element_type=jnp.float32)
    value_half = pre_act[:, :channels]
    gate_sig = jax.nn.sigmoid(pre_act[:, channels:])
    glu_out = (value_half * gate_sig * live_col).astype(jnp.bfloat16)
    glu_float = lax.optimization_barrier(glu_out).astype(jnp.float32)
    conv_out = jnp.zeros((frames_dev, channels), jnp.float32)
    for tap_index in range(tap_count):
        conv_out = conv_out + depthwise[tap_index] * tap_term(
            glu_float, owner_id, live_col, tap_index - radius
        )
    sum_val, sum_sq = small_sum(
        jnp.stack([jnp.sum(conv_out, axis=0), jnp.sum(conv_out * conv_out, axis=0)])
    )
    mean_val = sum_val / frame_total
    square_mean = sum_sq / frame_total
    inv_std = lax.rsqrt(square_mean - mean_val * mean_val + 1e-05)
    normed = (conv_out - mean_val) * inv_std
    scaled = normed * bn_gain + bn_shift
    sig_scaled = jax.nn.sigmoid(scaled)
    hidden = (scaled * sig_scaled * live_col).astype(jnp.bfloat16)
    grad_hidden = jnp.dot(grad_out, proj_out, preferred_element_type=jnp.float32) * live_col
    grad_scaled = grad_hidden * sig_scaled * (1.0 + scaled * (1.0 - sig_scaled))
    local_shift = jnp.sum(grad_scaled, axis=0)
    local_gain = jnp.sum(grad_scaled * normed, axis=0)
    shift_grad, gain_grad = small_sum(jnp.stack([local_shift, local_gain]))
    grad_conv = (
        live_col
        * bn_gain
        * inv_std
        * (grad_scaled - shift_grad / frame_total - normed * gain_grad / frame_total)
    )
    depth_rows = []
    for tap_index in range(tap_count):
        depth_rows.append(
            jnp.sum(grad_conv * tap_term(glu_float, owner_id, live_col, tap_index - radius), axis=0)
        )
    depth_grad = lax.psum(lax.psum(lax.psum(jnp.stack(depth_rows), "core"), "y"), "z")
    grad_glu = jnp.zeros((frames_dev, channels), jnp.float32)
    for tap_index in range(tap_count):
        offset = tap_index - radius
        back_same = (time_shift(owner_id, -offset, -1) == owner_id).astype(jnp.float32)[
            :, None
        ] * live_col
        grad_glu = grad_glu + depthwise[tap_index] * time_shift(grad_conv, -offset, 0.0) * back_same
    grad_value = grad_glu * gate_sig
    grad_gate = grad_glu * value_half * gate_sig * (1.0 - gate_sig)
    grad_flat = jnp.concatenate([grad_value, grad_gate], axis=1).astype(jnp.bfloat16)
    frame_term = lax.dot_general(
        proj_flat, grad_flat, (((1,), (1,)), ((), ())), preferred_element_type=jnp.float32
    ).T.astype(jnp.bfloat16)
    frame_parts = frame_term.reshape(frames_dev, groups, model_width // groups)
    frame_parts = lax.all_to_all(jnp.swapaxes(frame_parts, 0, 1), "mp", 0, 0)
    frame_grad = jnp.sum(frame_parts.astype(jnp.float32), axis=0).astype(jnp.bfloat16)
    summed = scatter_sum(
        jnp.concatenate(
            [
                lax.dot_general(
                    frames, grad_flat, (((0,), (0,)), ((), ())), preferred_element_type=jnp.float32
                ),
                lax.dot_general(
                    grad_out, hidden, (((0,), (0,)), ((), ())), preferred_element_type=jnp.float32
                ),
            ],
            axis=1,
        )
    )
    in_flat = summed[:, : 2 * channels]
    out_grad = summed[:, 2 * channels :]
    in_grad = in_flat.reshape(rows_dev, 2, channels)
    return (frame_grad, in_grad, out_grad, depth_grad, gain_grad, shift_grad)


def solution(mesh):
    grid = Mesh(mesh.devices.reshape(8, 8, 2, 4), ("y", "z", "core", "mp"))
    placed = (
        P(DP, None),
        P(None, None, "mp"),
        P(None, "mp"),
        P("mp"),
        P("mp"),
        P(None, "mp"),
        P(DP, None),
        P(),
        P(DP, None),
    )
    return jax.shard_map(
        shards,
        mesh=grid,
        in_specs=placed,
        out_specs=(
            P(DP, "mp"),
            P(DP, None, "mp"),
            P(DP, "mp"),
            P(None, "mp"),
            P("mp"),
            P("mp"),
        ),
        check_vma=False,
    )
```

```python
import functools

import jax
import jax.numpy as jnp
from jax import lax
from jax.experimental import pallas as pl
from jax.experimental.pallas import tpu as pltpu
from jax.sharding import Mesh, PartitionSpec as P

BLOCK = 128
DP = ("y", "z", "core")
YZ = ("y", "z")
LANES = 128
PAD = 16
F32 = jnp.float32
BF16 = jnp.bfloat16
VM = pl.BlockSpec(memory_space=pltpu.VMEM)
SM = pl.BlockSpec(memory_space=pltpu.SMEM)
NT = (((1,), (1,)), ((), ()))


def call(body, outs, ins, scratch=(), name=None):
    return pl.pallas_call(
        body,
        out_shape=outs,
        in_specs=ins,
        out_specs=jax.tree.map(lambda _: VM, outs),
        scratch_shapes=list(scratch),
        name=name,
    )


def shape(dims, dtype=F32):
    return jax.ShapeDtypeStruct(dims, dtype)


def lanes(h):
    return slice(h * LANES, (h + 1) * LANES)


def row_masks(len_ref, rows):
    row = lax.broadcasted_iota(jnp.int32, (rows, LANES), 0)
    split = len_ref[0, 0]
    end = split + len_ref[0, 1]
    return row < split, row < end


def embed(buf, h, x, first):
    rows = x.shape[0]
    zero = jnp.zeros((PAD, LANES), F32)
    head = jnp.where(first, x, 0.0)
    tail = jnp.where(first, 0.0, x)
    buf[h, 0:PAD] = zero
    buf[h, PAD : 2 * PAD] = head[:PAD]
    buf[h, 2 * PAD : PAD + rows] = head[PAD:] + tail[: rows - PAD]
    buf[h, PAD + rows : 2 * PAD + rows] = tail[rows - PAD :]
    buf[h, 2 * PAD + rows : 3 * PAD + rows] = zero


def conv(buf, h, taps, rows, first, sign):
    count = taps.shape[0]
    radius = count // 2
    span = rows + PAD
    total = jnp.zeros((span, LANES), F32)
    for k in range(count):
        total = total + taps[k : k + 1, lanes(h)] * buf[h, pl.ds(PAD + sign * (k - radius), span), :]
    return jnp.where(first, total[:rows], total[PAD:])


def tap_sums(out, values, buf, h, count, rows):
    radius = count // 2
    span = rows + PAD
    for k in range(count):
        prod = values * buf[h, pl.ds(PAD + k - radius, span), :]
        out[k : k + 1, lanes(h)] = jnp.sum(prod, axis=0, keepdims=True)


def forward_kernel(len_ref, frames, proj, taps, value, sig, buf, conv_out, pay):
    rows, channels = value.shape
    first, live = row_masks(len_ref, rows)
    pre = jnp.dot(frames[...], proj[...], preferred_element_type=F32)
    value[...] = pre[:, :channels]
    sig[...] = jax.nn.sigmoid(pre[:, channels:])
    sums = []
    for h in range(channels // LANES):
        glu = jnp.where(live, value[:, lanes(h)] * sig[:, lanes(h)], 0.0)
        embed(buf, h, glu.astype(BF16).astype(F32), first)
        out = jnp.where(live, conv(buf, h, taps, rows, first, 1), 0.0)
        conv_out[:, lanes(h)] = out
        sums.append(
            jnp.concatenate(
                [jnp.sum(out, axis=0, keepdims=True), jnp.sum(out * out, axis=0, keepdims=True)], axis=0
            )
        )
    both = jnp.concatenate(sums, axis=1)
    pay[...] = jnp.broadcast_to(both[None], pay.shape)


def side_kernel(len_ref, grad_out, proj_out, conv_out, buf, grad_hidden, ones_sum, conv_sum, work):
    rows, channels = grad_hidden.shape
    count = 31
    first, live = row_masks(len_ref, rows)
    hid = jnp.dot(grad_out[...], proj_out[...], preferred_element_type=F32)
    for h in range(channels // LANES):
        grad_hidden[:, lanes(h)] = jnp.where(live, hid[:, lanes(h)], 0.0)
        embed(work, h, jnp.where(live, 1.0, 0.0), first)
        tap_sums(ones_sum, work[h, pl.ds(PAD, rows + PAD), :], buf, h, count, rows)
        embed(work, h, conv_out[:, lanes(h)], first)
        tap_sums(conv_sum, work[h, pl.ds(PAD, rows + PAD), :], buf, h, count, rows)
        ones_sum[count : count + 1, lanes(h)] = jnp.zeros((1, LANES), F32)
        conv_sum[count : count + 1, lanes(h)] = jnp.zeros((1, LANES), F32)


def norm_kernel(
    len_ref, counts, got, gain, shift, conv_out, grad_hidden, buf, ones_sum, conv_sum,
    hidden, normed, grad_scaled, stats, pay, work, own_sum,
):
    rows, channels = conv_out.shape
    count = 31
    first, live = row_masks(len_ref, rows)
    total = jnp.sum(counts[...].astype(F32), axis=1, keepdims=True) * BLOCK
    sums = jnp.sum(got[...], axis=0)
    mean = sums[0:1] / total
    inv_std = lax.rsqrt(sums[1:2] / total - mean * mean + 1e-05)
    stats[0:1] = mean
    stats[1:2] = inv_std
    heads = []
    for h in range(channels // LANES):
        cols = lanes(h)
        norm = (conv_out[:, cols] - mean[:, cols]) * inv_std[:, cols]
        scaled = norm * gain[:, cols] + shift[:, cols]
        s = jax.nn.sigmoid(scaled)
        hidden[:, cols] = jnp.where(live, scaled * s, 0.0).astype(BF16)
        grad = grad_hidden[:, cols] * s * (1.0 + scaled * (1.0 - s))
        normed[:, cols] = norm
        grad_scaled[:, cols] = grad
        heads.append((jnp.sum(grad, axis=0, keepdims=True), jnp.sum(grad * norm, axis=0, keepdims=True)))
        embed(work, h, grad, first)
        tap_sums(own_sum, work[h, pl.ds(PAD, rows + PAD), :], buf, h, count, rows)
        own_sum[count : count + 1, cols] = jnp.zeros((1, LANES), F32)
    (s0, q0), (s1, q1) = heads
    tile = jnp.concatenate([s0, s1, q0, q1, jnp.zeros((4, LANES), F32)], axis=0)
    pay[...] = jnp.broadcast_to(tile[None], pay.shape)
    for j in range(pay.shape[0] // 2):
        k, cols = j // 2, lanes(j % 2)
        for i, ref in enumerate((own_sum, ones_sum, conv_sum)):
            part = ref[k : k + 1, cols]
            pay[2 * j, 4 + i : 5 + i, :] = part
            pay[2 * j + 1, 4 + i : 5 + i, :] = part


def back_kernel(
    len_ref, half_ref, counts, got, gain, stats, normed, grad_scaled, value, sig, taps,
    grad_pre, shift_grad, gain_grad, slice_out, work,
):
    rows, channels = normed.shape
    first, live = row_masks(len_ref, rows)
    total = jnp.sum(counts[...].astype(F32), axis=1, keepdims=True) * BLOCK
    sums = jnp.sum(got[...], axis=0)
    mean, inv_std = stats[0:1], stats[1:2]
    slices = []
    for h in range(channels // LANES):
        cols = lanes(h)
        s, q = sums[h : h + 1], sums[2 + h : 3 + h]
        shift_grad[:, cols] = s
        gain_grad[:, cols] = q
        scale = gain[:, cols] * inv_std[:, cols]
        grad = scale * (grad_scaled[:, cols] - s / total - normed[:, cols] * (q / total))
        embed(work, h, jnp.where(live, grad, 0.0), first)
        glu = jnp.where(live, conv(work, h, taps, rows, first, -1), 0.0)
        v, g = value[:, cols], sig[:, cols]
        grad_pre[:, cols] = (glu * g).astype(BF16)
        grad_pre[:, channels + h * LANES : channels + (h + 1) * LANES] = (glu * v * g * (1.0 - g)).astype(BF16)
        own, ones, cv = sums[4:5], sums[5:6], sums[6:7]
        slices.append(
            scale * (own - s / total * ones - q / total * inv_std[:, cols] * (cv - mean[:, cols] * ones))
        )
    which = jnp.full((1, LANES), half_ref[0], jnp.int32)
    depth = jnp.where(which == 0, slices[0], slices[1])
    slice_out[...] = jnp.broadcast_to(depth, slice_out.shape)


def frame_kernel(mp_ref, grad_pre, proj, own, one, two, three):
    width = own.shape[1]
    groups = proj.shape[0] // width
    for d, out in enumerate((own, one, two, three)):
        at = pl.multiple_of(lax.rem(mp_ref[0] + d, groups) * width, width)
        term = lax.dot_general(grad_pre[...], proj[pl.ds(at, width), :], NT, preferred_element_type=F32)
        out[...] = term.astype(BF16)


def rows_kernel(left, own, other, out):
    tokens = own.shape[0]
    total = jnp.dot(left[:, :tokens], own[...], preferred_element_type=F32)
    total = total + jnp.dot(left[:, tokens:], other[...], preferred_element_type=F32)
    out[...] = total.astype(BF16)


def bulk_kernel(left, own, other, out_rows, depth, pay):
    tokens, width = own.shape
    peers, rows, _ = pay.shape
    total = jnp.dot(left[:, :tokens], own[...], preferred_element_type=F32)
    total = total + jnp.dot(left[:, tokens:], other[...], preferred_element_type=F32)
    pay[:, :, :width] = total.reshape(peers, rows, width).astype(BF16)
    pay[:, :, width : width + out_rows.shape[2]] = out_rows[...]
    pay[:, :, width + out_rows.shape[2] :] = jnp.broadcast_to(
        depth[...].astype(BF16)[None], (peers, rows, LANES)
    )


def last_kernel(got, in_rows, out_rows, depth):
    width, more = in_rows.shape[1], out_rows.shape[1]
    in_rows[...] = jnp.sum(got[:, :, :width].astype(F32), axis=0)
    out_rows[...] = jnp.sum(got[:, :, width : width + more].astype(F32), axis=0)
    for j in range(2 * depth.shape[0]):
        depth[j // 2 : j // 2 + 1, lanes(j % 2)] = got[j, 0:1, width + more :].astype(F32)


def core_halves(x, core):
    frames, width = x.shape
    parts = x.T.reshape(width // 16, 2, 8, frames)
    keep = lax.dynamic_index_in_dim(parts, core, 1, keepdims=False).reshape(width // 2, frames)
    send = lax.dynamic_index_in_dim(parts, 1 - core, 1, keepdims=False).reshape(width // 2, frames)
    return keep, send


def swap_cores(x):
    return lax.ppermute(x, "core", [(0, 1), (1, 0)])


def after(x, y):
    return lax.optimization_barrier((x, y))[0]


def shards(frames, proj_in, taps, bn_gain, bn_shift, proj_out, grad_out, counts, lengths):
    rows, width = frames.shape
    channels = proj_in.shape[2]
    count = taps.shape[0]
    halves = channels // LANES
    buf_rows = rows + 3 * PAD
    peers = lax.axis_size(DP)
    chips = lax.axis_size(YZ)
    groups = lax.axis_size("mp")
    rows_dev = width // peers
    core = lax.axis_index("core")
    chip = lax.axis_index(YZ)
    mp = lax.axis_index("mp")
    full = shape((rows, channels))
    proj = proj_in.reshape(width, 2 * channels)
    counts_row = counts.reshape(1, -1)
    gain_row = bn_gain.reshape(1, channels)
    shift_row = bn_shift.reshape(1, channels)

    value, sig, buf, conv_out, pay = call(
        forward_kernel,
        (full, full, shape((halves, buf_rows, LANES)), full, shape((peers, 2, channels))),
        [SM, VM, VM, VM],
        name="forward",
    )(lengths, frames, proj, taps)
    got = lax.all_to_all(pay, DP, 0, 0)

    grad_hidden, ones_sum, conv_sum = call(
        side_kernel,
        (full, shape((count + 1, channels)), shape((count + 1, channels))),
        [SM, VM, VM, VM, VM],
        [pltpu.VMEM((halves, buf_rows, LANES), F32)],
        name="side",
    )(lengths, grad_out, proj_out, conv_out, buf)
    left_in = core_halves(frames, core)
    left_out = core_halves(grad_out, core)
    left_in = jnp.concatenate([left_in[0], swap_cores(after(left_in[1], pay))], axis=1)
    left_out = jnp.concatenate([left_out[0], swap_cores(after(left_out[1], pay))], axis=1)

    hidden, normed, grad_scaled, stats, pay = call(
        norm_kernel,
        (
            shape((rows, channels), BF16),
            full,
            full,
            shape((2, channels)),
            shape((peers, 8, LANES)),
        ),
        [SM] + [VM] * 9,
        [pltpu.VMEM((halves, buf_rows, LANES), F32), pltpu.VMEM((count + 1, channels), F32)],
        name="norm",
    )(lengths, counts_row, got, gain_row, shift_row, conv_out, grad_hidden, buf, ones_sum, conv_sum)
    got = lax.all_to_all(pay, DP, 0, 0)

    other = swap_cores(after(hidden, pay))
    out_rows = call(rows_kernel, shape((width // 2, channels), BF16), [VM] * 3, name="out_rows")(
        left_out, hidden, other
    ).reshape(chips, rows_dev, channels)

    half = (chip % 2).astype(jnp.int32).reshape(1)
    grad_pre, shift_grad, gain_grad, depth = call(
        back_kernel,
        (
            shape((rows, 2 * channels), BF16),
            shape((1, channels)),
            shape((1, channels)),
            shape((rows_dev, LANES)),
        ),
        [SM, SM] + [VM] * 9,
        [pltpu.VMEM((halves, buf_rows, LANES), F32)],
        name="back",
    )(lengths, half, counts_row, got, gain_row, stats, normed, grad_scaled, value, sig, taps)

    other = swap_cores(grad_pre)
    term = shape((rows, width // groups), BF16)
    own, one, two, three = call(frame_kernel, (term,) * 4, [SM, VM, VM], name="frame")(
        mp.astype(jnp.int32).reshape(1), grad_pre, proj
    )
    pay = call(
        bulk_kernel,
        shape((chips, rows_dev, 3 * channels + LANES), BF16),
        [VM] * 5,
        name="bulk",
    )(left_in, grad_pre, other, out_rows, depth)
    got = lax.all_to_all(pay, YZ, 0, 0)

    frame_sum = own.astype(F32)
    for d, part in ((1, one), (2, two), (3, three)):
        part = lax.ppermute(after(part, pay), "mp", [(i, (i + d) % groups) for i in range(groups)])
        frame_sum = frame_sum + part.astype(F32)
    frame_grad = frame_sum.astype(BF16)

    in_rows, out_grad, depth_grad = call(
        last_kernel,
        (shape((rows_dev, 2 * channels)), shape((rows_dev, channels)), shape((count, channels))),
        [VM],
        name="last",
    )(got)
    in_grad = in_rows.reshape(rows_dev, 2, channels)
    return (frame_grad, in_grad, out_grad, depth_grad, gain_grad.reshape(channels), shift_grad.reshape(channels))


def solution(mesh):
    grid = Mesh(mesh.devices.reshape(8, 8, 2, 4), ("y", "z", "core", "mp"))
    placed = (
        P(DP, None),
        P(None, None, "mp"),
        P(None, "mp"),
        P("mp"),
        P("mp"),
        P(None, "mp"),
        P(DP, None),
        P(),
        P(DP, None),
    )
    return jax.shard_map(
        shards,
        mesh=grid,
        in_specs=placed,
        out_specs=(
            P(DP, "mp"),
            P(DP, None, "mp"),
            P(DP, "mp"),
            P(None, "mp"),
            P("mp"),
            P("mp"),
        ),
        check_vma=False,
    )
```

```python
import functools

import jax
import jax.numpy as jnp
from jax import lax
from jax.experimental import pallas as pl
from jax.experimental.pallas import tpu as pltpu
from jax.sharding import Mesh, PartitionSpec as P

BLOCK = 128
DP = ("y", "z", "core")
YZ = ("y", "z")
LANES = 128
PAD = 16
F32 = jnp.float32
BF16 = jnp.bfloat16
VM = pl.BlockSpec(memory_space=pltpu.VMEM)
SM = pl.BlockSpec(memory_space=pltpu.SMEM)
NT = (((1,), (1,)), ((), ()))


def call(body, outs, ins, scratch=(), name=None):
    kernel = pl.pallas_call(
        body,
        out_shape=outs,
        in_specs=ins,
        out_specs=tuple(VM for _ in outs),
        scratch_shapes=list(scratch),
        name=name,
    )

    def run(*args):
        held = [
            pltpu.with_memory_space_constraint(a, pltpu.VMEM) if spec is VM else a
            for a, spec in zip(args, ins)
        ]
        return kernel(*held)

    return run


def shape(dims, dtype=F32):
    return pltpu.VMEM(dims, dtype)


def hbm_shape(dims, dtype=F32):
    return jax.ShapeDtypeStruct(dims, dtype)


def tree_sum(x):
    while x.shape[0] > 1:
        half = x.shape[0] // 2
        x = x[:half] + x[half:]
    return x[0]


def lanes(h):
    return slice(h * LANES, (h + 1) * LANES)


def row_masks(len_ref, rows):
    row = lax.broadcasted_iota(jnp.int32, (rows, LANES), 0)
    split = len_ref[0, 0]
    end = split + len_ref[0, 1]
    return row < split, row < end


def embed(buf, h, x, first):
    rows = x.shape[0]
    zero = jnp.zeros((PAD, LANES), F32)
    head = jnp.where(first, x, 0.0)
    tail = jnp.where(first, 0.0, x)
    buf[h, 0:PAD] = zero
    buf[h, PAD : 2 * PAD] = head[:PAD]
    buf[h, 2 * PAD : PAD + rows] = head[PAD:] + tail[: rows - PAD]
    buf[h, PAD + rows : 2 * PAD + rows] = tail[rows - PAD :]
    buf[h, 2 * PAD + rows : 3 * PAD + rows] = zero


def conv(buf, h, taps, rows, first, sign):
    count = taps.shape[0]
    radius = count // 2
    span = rows + PAD
    total = jnp.zeros((span, LANES), F32)
    for k in range(count):
        total = total + taps[k : k + 1, lanes(h)] * buf[h, pl.ds(PAD + sign * (k - radius), span), :]
    return jnp.where(first, total[:rows], total[PAD:])


def tap_sums(out, values, buf, h, count, rows):
    radius = count // 2
    span = rows + PAD
    for k in range(count):
        prod = values * buf[h, pl.ds(PAD + k - radius, span), :]
        out[k : k + 1, lanes(h)] = jnp.sum(prod, axis=0, keepdims=True)


def forward_kernel(len_ref, frames, proj, taps, value, sig, buf, conv_out, pay):
    rows, channels = value.shape
    first, live = row_masks(len_ref, rows)
    pre = jnp.dot(frames[...], proj[...], preferred_element_type=F32)
    value[...] = pre[:, :channels]
    sig[...] = jax.nn.sigmoid(pre[:, channels:])
    sums = []
    for h in range(channels // LANES):
        glu = jnp.where(live, value[:, lanes(h)] * sig[:, lanes(h)], 0.0)
        embed(buf, h, glu.astype(BF16).astype(F32), first)
        out = jnp.where(live, conv(buf, h, taps, rows, first, 1), 0.0)
        conv_out[:, lanes(h)] = out
        sums.append(
            jnp.concatenate(
                [jnp.sum(out, axis=0, keepdims=True), jnp.sum(out * out, axis=0, keepdims=True)], axis=0
            )
        )
    both = jnp.concatenate(sums, axis=1)
    pay[...] = jnp.broadcast_to(both[None], pay.shape)


def side_kernel(len_ref, grad_out, proj_out, conv_out, buf, grad_hidden, ones_sum, conv_sum, work):
    rows, channels = grad_hidden.shape
    count = 31
    first, live = row_masks(len_ref, rows)
    hid = jnp.dot(grad_out[...], proj_out[...], preferred_element_type=F32)
    for h in range(channels // LANES):
        grad_hidden[:, lanes(h)] = jnp.where(live, hid[:, lanes(h)], 0.0)
        embed(work, h, jnp.where(live, 1.0, 0.0), first)
        tap_sums(ones_sum, work[h, pl.ds(PAD, rows + PAD), :], buf, h, count, rows)
        embed(work, h, conv_out[:, lanes(h)], first)
        tap_sums(conv_sum, work[h, pl.ds(PAD, rows + PAD), :], buf, h, count, rows)
        ones_sum[count : count + 1, lanes(h)] = jnp.zeros((1, LANES), F32)
        conv_sum[count : count + 1, lanes(h)] = jnp.zeros((1, LANES), F32)


def norm_kernel(
    len_ref, counts, got, gain, shift, conv_out, grad_hidden, buf, ones_sum, conv_sum,
    hidden, normed, grad_scaled, stats, sums_out, work,
):
    rows, channels = conv_out.shape
    count = 31
    first, live = row_masks(len_ref, rows)
    total = jnp.sum(counts[...].astype(F32), axis=1, keepdims=True) * BLOCK
    sums = tree_sum(got[...])
    mean = sums[0:1] / total
    inv_std = lax.rsqrt(sums[1:2] / total - mean * mean + 1e-05)
    stats[0:1] = mean
    stats[1:2] = inv_std
    heads = []
    for h in range(channels // LANES):
        cols = lanes(h)
        norm = (conv_out[:, cols] - mean[:, cols]) * inv_std[:, cols]
        scaled = norm * gain[:, cols] + shift[:, cols]
        s = jax.nn.sigmoid(scaled)
        hidden[:, cols] = jnp.where(live, scaled * s, 0.0).astype(BF16)
        grad = grad_hidden[:, cols] * s * (1.0 + scaled * (1.0 - s))
        normed[:, cols] = norm
        grad_scaled[:, cols] = grad
        heads.append((jnp.sum(grad, axis=0, keepdims=True), jnp.sum(grad * norm, axis=0, keepdims=True)))
        embed(work, h, grad, first)
        tap_sums(sums_out, work[h, pl.ds(PAD, rows + PAD), :], buf, h, count, rows)
        sums_out[count : count + 1, cols] = jnp.zeros((1, LANES), F32)
    (s0, q0), (s1, q1) = heads
    base = 3 * (count + 1)
    for i, ref in enumerate((ones_sum, conv_sum)):
        sums_out[(i + 1) * (count + 1) : (i + 2) * (count + 1)] = ref[...]
    sums_out[base : base + 1] = jnp.concatenate([s0, s1], axis=1)
    sums_out[base + 1 : base + 2] = jnp.concatenate([q0, q1], axis=1)
    sums_out[base + 2 :] = jnp.zeros((6, channels), F32)


def spread_kernel(own, other, pay, sums):
    sums[...] = own[...] + other[...]
    count = pay.shape[0] // 2
    base = 3 * count
    tile = jnp.concatenate(
        [sums[base + i : base + i + 1, lanes(h)] for i in range(2) for h in range(2)]
        + [jnp.zeros((4, LANES), F32)],
        axis=0,
    )
    pay[...] = jnp.broadcast_to(tile[None], pay.shape)
    for j in range(pay.shape[0]):
        for i in range(3):
            at = i * count + j // 2
            pay[j, 4 + i : 5 + i, :] = sums[at : at + 1, lanes(j % 2)]


def back_kernel(
    len_ref, half_ref, counts, got, gain, stats, normed, grad_scaled, value, sig, taps,
    grad_pre, shift_grad, gain_grad, slice_out, work,
):
    rows, channels = normed.shape
    first, live = row_masks(len_ref, rows)
    total = jnp.sum(counts[...].astype(F32), axis=1, keepdims=True) * BLOCK
    sums = tree_sum(got[...])
    mean, inv_std = stats[0:1], stats[1:2]
    slices = []
    for h in range(channels // LANES):
        cols = lanes(h)
        s, q = sums[h : h + 1], sums[2 + h : 3 + h]
        shift_grad[:, cols] = s
        gain_grad[:, cols] = q
        scale = gain[:, cols] * inv_std[:, cols]
        grad = scale * (grad_scaled[:, cols] - s / total - normed[:, cols] * (q / total))
        embed(work, h, jnp.where(live, grad, 0.0), first)
        glu = jnp.where(live, conv(work, h, taps, rows, first, -1), 0.0)
        v, g = value[:, cols], sig[:, cols]
        grad_pre[:, cols] = (glu * g).astype(BF16)
        grad_pre[:, channels + h * LANES : channels + (h + 1) * LANES] = (glu * v * g * (1.0 - g)).astype(BF16)
        own, ones, cv = sums[4:5], sums[5:6], sums[6:7]
        slices.append(
            scale * (own - s / total * ones - q / total * inv_std[:, cols] * (cv - mean[:, cols] * ones))
        )
    which = jnp.full((1, LANES), half_ref[0], jnp.int32)
    depth = jnp.where(which == 0, slices[0], slices[1])
    slice_out[...] = jnp.broadcast_to(depth, slice_out.shape)


def frame_kernel(mp_ref, grad_pre, proj, own, one, two, three):
    width = own.shape[1]
    groups = proj.shape[0] // width
    for d, out in enumerate((own, one, two, three)):
        at = pl.multiple_of(lax.rem(mp_ref[0] + d, groups) * width, width)
        term = lax.dot_general(grad_pre[...], proj[pl.ds(at, width), :], NT, preferred_element_type=F32)
        out[...] = term.astype(BF16)


def rows_kernel(left_own, left_other, own, other, out):
    total = jnp.dot(left_own[...], own[...], preferred_element_type=F32)
    total = total + jnp.dot(left_other[...], other[...], preferred_element_type=F32)
    out[...] = total.astype(BF16)


def bulk_kernel(left_own, left_other, own, other, out_rows, depth, pay):
    width = own.shape[1]
    peers, rows, _ = pay.shape
    total = jnp.dot(left_own[...], own[...], preferred_element_type=F32)
    total = total + jnp.dot(left_other[...], other[...], preferred_element_type=F32)
    pay[:, :, :width] = total.reshape(peers, rows, width).astype(BF16)
    pay[:, :, width : width + out_rows.shape[2]] = out_rows[...]
    pay[:, :, width + out_rows.shape[2] :] = jnp.broadcast_to(
        depth[...].astype(BF16)[None], (peers, rows, LANES)
    )


def last_kernel(got, in_rows, out_rows, depth):
    more = out_rows.shape[1]
    width = 2 * more
    for g in range(2):
        total = jnp.zeros((in_rows.shape[0], more), F32)
        for j in range(got.shape[0]):
            total = total + got[j, :, g * more : (g + 1) * more].astype(F32)
        in_rows[:, g, :] = total
    total = jnp.zeros((in_rows.shape[0], more), F32)
    for j in range(got.shape[0]):
        total = total + got[j, :, width : width + more].astype(F32)
    out_rows[...] = total
    for j in range(2 * depth.shape[0]):
        depth[j // 2 : j // 2 + 1, lanes(j % 2)] = got[j, 0:1, width + more :].astype(F32)


def core_halves(x, core):
    frames, width = x.shape
    parts = x.T.reshape(width // 16, 2, 8, frames)
    keep = lax.dynamic_index_in_dim(parts, core, 1, keepdims=False).reshape(width // 2, frames)
    send = lax.dynamic_index_in_dim(parts, 1 - core, 1, keepdims=False).reshape(width // 2, frames)
    return keep, send


def swap_cores(x):
    return lax.ppermute(x, "core", [(0, 1), (1, 0)])


def after(x, y):
    return lax.optimization_barrier((x, y))[0]


def shards(frames, proj_in, taps, bn_gain, bn_shift, proj_out, grad_out, counts, lengths):
    rows, width = frames.shape
    channels = proj_in.shape[2]
    count = taps.shape[0]
    halves = channels // LANES
    buf_rows = rows + 3 * PAD
    peers = lax.axis_size(DP)
    chips = lax.axis_size(YZ)
    groups = lax.axis_size("mp")
    rows_dev = width // peers
    core = lax.axis_index("core")
    chip = lax.axis_index(YZ)
    mp = lax.axis_index("mp")
    full = shape((rows, channels))
    proj = proj_in.reshape(width, 2 * channels)
    counts_row = counts.reshape(1, -1)
    gain_row = bn_gain.reshape(1, channels)
    shift_row = bn_shift.reshape(1, channels)

    value, sig, buf, conv_out, pay = call(
        forward_kernel,
        (full, full, shape((halves, buf_rows, LANES)), full, hbm_shape((peers, 2, channels))),
        [SM, VM, VM, VM],
        name="forward",
    )(lengths, frames, proj, taps)
    got = lax.all_to_all(pay, DP, 0, 0)

    grad_hidden, ones_sum, conv_sum = call(
        side_kernel,
        (full, shape((count + 1, channels)), shape((count + 1, channels))),
        [SM, VM, VM, VM, VM],
        [pltpu.VMEM((halves, buf_rows, LANES), F32)],
        name="side",
    )(lengths, grad_out, proj_out, conv_out, buf)
    left_in, send_in = core_halves(frames, core)
    left_out, send_out = core_halves(grad_out, core)
    other_in = swap_cores(after(send_in, pay))
    other_out = swap_cores(after(send_out, pay))

    tap_rows = 3 * (count + 1)
    hidden, normed, grad_scaled, stats, sums = call(
        norm_kernel,
        (
            shape((rows, channels), BF16),
            full,
            full,
            shape((2, channels)),
            shape((tap_rows + 8, channels)),
        ),
        [SM] + [VM] * 9,
        [pltpu.VMEM((halves, buf_rows, LANES), F32)],
        name="norm",
    )(lengths, counts_row, got, gain_row, shift_row, conv_out, grad_hidden, buf, ones_sum, conv_sum)
    (pay,) = call(
        spread_kernel,
        (hbm_shape((chips, 8, LANES)),),
        [VM, VM],
        [pltpu.VMEM((tap_rows + 8, channels), F32)],
        name="spread",
    )(sums, swap_cores(sums))
    got = lax.all_to_all(pay, YZ, 0, 0)

    other = swap_cores(after(hidden, pay))
    (out_rows,) = call(rows_kernel, (shape((width // 2, channels), BF16),), [VM] * 4, name="out_rows")(
        left_out, other_out, hidden, other
    )
    got, out_rows, other_in = lax.optimization_barrier((got, out_rows, other_in))
    out_rows = out_rows.reshape(chips, rows_dev, channels)

    half = (chip % 2).astype(jnp.int32).reshape(1)
    grad_pre, shift_grad, gain_grad, depth = call(
        back_kernel,
        (
            shape((rows, 2 * channels), BF16),
            shape((1, channels)),
            shape((1, channels)),
            shape((rows_dev, LANES)),
        ),
        [SM, SM] + [VM] * 9,
        [pltpu.VMEM((halves, buf_rows, LANES), F32)],
        name="back",
    )(lengths, half, counts_row, got, gain_row, stats, normed, grad_scaled, value, sig, taps)

    other = swap_cores(grad_pre)
    term = shape((rows, width // groups), BF16)
    own, one, two, three = call(frame_kernel, (term,) * 4, [SM, VM, VM], name="frame")(
        mp.astype(jnp.int32).reshape(1), grad_pre, proj
    )
    (pay,) = call(
        bulk_kernel,
        (hbm_shape((chips, rows_dev, 3 * channels + LANES), BF16),),
        [VM] * 6,
        name="bulk",
    )(left_in, other_in, grad_pre, other, out_rows, depth)
    got = lax.all_to_all(pay, YZ, 0, 0)

    frame_sum = own.astype(F32)
    for d, part in ((1, one), (2, two), (3, three)):
        part = lax.ppermute(after(part, pay), "mp", [(i, (i + d) % groups) for i in range(groups)])
        frame_sum = frame_sum + part.astype(F32)
    frame_grad = frame_sum.astype(BF16)

    in_grad, out_grad, depth_grad = call(
        last_kernel,
        (hbm_shape((rows_dev, 2, channels)), hbm_shape((rows_dev, channels)), hbm_shape((count, channels))),
        [VM],
        name="last",
    )(got)
    return (frame_grad, in_grad, out_grad, depth_grad, gain_grad.reshape(channels), shift_grad.reshape(channels))


def solution(mesh):
    grid = Mesh(mesh.devices.reshape(8, 8, 2, 4), ("y", "z", "core", "mp"))
    placed = (
        P(DP, None),
        P(None, None, "mp"),
        P(None, "mp"),
        P("mp"),
        P("mp"),
        P(None, "mp"),
        P(DP, None),
        P(),
        P(DP, None),
    )
    return jax.shard_map(
        shards,
        mesh=grid,
        in_specs=placed,
        out_specs=(
            P(DP, "mp"),
            P(DP, None, "mp"),
            P(DP, "mp"),
            P(None, "mp"),
            P("mp"),
            P("mp"),
        ),
        check_vma=False,
    )
```

```python
import functools

import jax
import jax.numpy as jnp
from jax import lax
from jax.experimental import pallas as pl
from jax.experimental.pallas import tpu as pltpu
from jax.sharding import Mesh, PartitionSpec as P

BLOCK = 128
DP = ("y", "z", "core")
YZ = ("y", "z")
LANES = 128
TAPS = 31
PAD = 16
F32 = jnp.float32
BF16 = jnp.bfloat16
VM = pl.BlockSpec(memory_space=pltpu.VMEM)
HB = pl.BlockSpec(memory_space=pltpu.VMEM)
SM = pl.BlockSpec(memory_space=pltpu.SMEM)
NT = (((1,), (1,)), ((), ()))


def call(body, outs, ins, scratch=(), name=None):
    kernel = pl.pallas_call(
        body,
        out_shape=outs,
        in_specs=ins,
        out_specs=tuple(VM for _ in outs),
        scratch_shapes=list(scratch),
        name=name,
    )

    def run(*args):
        held = [
            pltpu.with_memory_space_constraint(a, pltpu.VMEM) if spec is VM else a
            for a, spec in zip(args, ins)
        ]
        return kernel(*held)

    return run


def shape(dims, dtype=F32):
    return pltpu.VMEM(dims, dtype)


def hbm_shape(dims, dtype=F32):
    return jax.ShapeDtypeStruct(dims, dtype)


def tree_sum(x):
    while x.shape[0] > 1:
        half = x.shape[0] // 2
        x = x[:half] + x[half:]
    return x[0]


def lanes(h):
    return slice(h * LANES, (h + 1) * LANES)


def row_masks(split, end, rows):
    row = lax.broadcasted_iota(jnp.int32, (rows, LANES), 0).astype(F32)
    return row < split, row < end


def own_masks(len_ref, rows):
    split = len_ref[0, 0]
    return row_masks(split.astype(F32), (split + len_ref[0, 1]).astype(F32), rows)


def embed(buf, h, x, first):
    rows = x.shape[0]
    zero = jnp.zeros((PAD, LANES), F32)
    head = jnp.where(first, x, 0.0)
    tail = jnp.where(first, 0.0, x)
    buf[h, 0:PAD] = zero
    buf[h, PAD : 2 * PAD] = head[:PAD]
    buf[h, 2 * PAD : PAD + rows] = head[PAD:] + tail[: rows - PAD]
    buf[h, PAD + rows : 2 * PAD + rows] = tail[rows - PAD :]
    buf[h, 2 * PAD + rows : 3 * PAD + rows] = zero


def conv(buf, h, taps, rows, first, sign):
    count = taps.shape[0]
    radius = count // 2
    span = rows + PAD
    total = jnp.zeros((span, LANES), F32)
    for k in range(count):
        total = total + taps[k : k + 1, lanes(h)] * buf[h, pl.ds(PAD + sign * (k - radius), span), :]
    return jnp.where(first, total[:rows], total[PAD:])


def tap_sums(out, values, buf, h, count, rows):
    radius = count // 2
    span = rows + PAD
    for k in range(count):
        prod = values * buf[h, pl.ds(PAD + k - radius, span), :]
        out[k : k + 1, lanes(h)] = jnp.sum(prod, axis=0, keepdims=True)


def gated(pre, live, h, channels):
    value = pre[:, lanes(h)]
    sig = jax.nn.sigmoid(pre[:, channels + h * LANES : channels + (h + 1) * LANES])
    return value, sig, jnp.where(live, value * sig, 0.0).astype(BF16).astype(F32)


def forward_kernel(len_ref, frames, proj, taps, conv_out, buf, pay, pre):
    rows, channels = conv_out.shape
    first, live = own_masks(len_ref, rows)
    pre[...] = jnp.dot(frames[...], proj[...], preferred_element_type=F32)
    sums = []
    for h in range(channels // LANES):
        _, _, glu = gated(pre, live, h, channels)
        embed(buf, h, glu, first)
        out = jnp.where(live, conv(buf, h, taps, rows, first, 1), 0.0)
        conv_out[:, lanes(h)] = out
        sums.append(
            jnp.concatenate(
                [jnp.sum(out, axis=0, keepdims=True), jnp.sum(out * out, axis=0, keepdims=True)], axis=0
            )
        )
    both = jnp.concatenate(sums, axis=1)
    pay[...] = jnp.broadcast_to(both[None], pay.shape)


def known_sums(ones_sum, conv_sum, conv_out, buf, work, h, rows, first, live):
    count = TAPS
    embed(work, h, jnp.where(live, 1.0, 0.0), first)
    tap_sums(ones_sum, work[h, pl.ds(PAD, rows + PAD), :], buf, h, count, rows)
    embed(work, h, conv_out[:, lanes(h)], first)
    tap_sums(conv_sum, work[h, pl.ds(PAD, rows + PAD), :], buf, h, count, rows)
    ones_sum[count : count + 1, lanes(h)] = jnp.zeros((1, LANES), F32)
    conv_sum[count : count + 1, lanes(h)] = jnp.zeros((1, LANES), F32)


def side_kernel(
    len_ref, frames, proj, grad_out, proj_out, conv_out, buf, gain, shift, counts,
    value, sig, grad_hidden, ones_sum, conv_sum, params, pre, hid, work,
):
    rows, channels = conv_out.shape
    first, live = own_masks(len_ref, rows)
    pre[...] = jnp.dot(frames[...], proj[...], preferred_element_type=F32)
    hid[...] = jnp.dot(grad_out[...], proj_out[...], preferred_element_type=F32)
    for h in range(channels // LANES):
        cols = lanes(h)
        value[:, cols], sig[:, cols], _ = gated(pre, live, h, channels)
        grad_hidden[:, cols] = jnp.where(live, hid[:, cols], 0.0)
        known_sums(ones_sum, conv_sum, conv_out, buf, work, h, rows, first, live)
    total = jnp.sum(counts[...].astype(F32), axis=1, keepdims=True) * BLOCK
    params[0:1] = gain[...]
    params[1:2] = shift[...]
    params[2:3] = jnp.broadcast_to(total, (1, channels))
    params[3:] = jnp.zeros((5, channels), F32)


def mirror_kernel(
    given, proj, proj_out, taps,
    value, sig, grad_hidden, ones_sum, conv_sum, conv_out, buf, ends, pre, hid, work,
):
    rows, channels = conv_out.shape
    spans = given[2 * rows : 2 * rows + 16, :LANES].astype(F32)[0:1]
    split = spans[:, 0:1]
    end = split + spans[:, 1:2]
    ends[0:1] = jnp.broadcast_to(split, (1, LANES))
    ends[1:2] = jnp.broadcast_to(end, (1, LANES))
    ends[2:] = jnp.zeros((6, LANES), F32)
    first, live = row_masks(ends[0:1], ends[1:2], rows)
    pre[...] = jnp.dot(given[:rows], proj[...], preferred_element_type=F32)
    hid[...] = jnp.dot(given[rows : 2 * rows], proj_out[...], preferred_element_type=F32)
    for h in range(channels // LANES):
        cols = lanes(h)
        value[:, cols], sig[:, cols], glu = gated(pre, live, h, channels)
        embed(buf, h, glu, first)
        conv_out[:, cols] = jnp.where(live, conv(buf, h, taps, rows, first, 1), 0.0)
        grad_hidden[:, cols] = jnp.where(live, hid[:, cols], 0.0)
        known_sums(ones_sum, conv_sum, conv_out, buf, work, h, rows, first, live)


def norm_kernel(
    len_ref, ends, got, params, conv_a, conv_b, hid_a, hid_b, buf_a, buf_b,
    ones_a, ones_b, conv_sum_a, conv_sum_b,
    hidden, grad_scaled, stats, pay, work, sums,
):
    rows, channels = conv_a.shape
    count = TAPS
    total = params[2:3]
    found = tree_sum(got[...])
    mean = found[0:1] / total
    inv_std = lax.rsqrt(found[1:2] / total - mean * mean + 1e-05)
    stats[0:1] = mean
    stats[1:2] = inv_std
    heads = []
    for h in range(channels // LANES):
        cols = lanes(h)
        head = []
        for part, (conv_out, grad_hidden, buf) in enumerate(((conv_a, hid_a, buf_a), (conv_b, hid_b, buf_b))):
            masks = own_masks(len_ref, rows) if part == 0 else row_masks(ends[0:1], ends[1:2], rows)
            first, live = masks
            span = slice(part * rows, (part + 1) * rows)
            norm = (conv_out[:, cols] - mean[:, cols]) * inv_std[:, cols]
            scaled = norm * params[0:1, cols] + params[1:2, cols]
            s = jax.nn.sigmoid(scaled)
            hidden[span, cols] = jnp.where(live, scaled * s, 0.0).astype(BF16)
            grad = grad_hidden[:, cols] * s * (1.0 + scaled * (1.0 - s))
            grad_scaled[span, cols] = grad
            head.append((jnp.sum(grad, axis=0, keepdims=True), jnp.sum(grad * norm, axis=0, keepdims=True)))
            embed(work, h, grad, first)
            tap_sums(sums.at[part], work[h, pl.ds(PAD, rows + PAD), :], buf, h, count, rows)
            sums[part, count : count + 1, cols] = jnp.zeros((1, LANES), F32)
        heads.append([a + b for a, b in zip(*head)])
    sums[0] = sums[0] + sums[1]
    sums[1] = ones_a[...] + ones_b[...]
    sums[2] = conv_sum_a[...] + conv_sum_b[...]
    (s0, q0), (s1, q1) = heads
    tile = jnp.concatenate([s0, s1, q0, q1, jnp.zeros((4, LANES), F32)], axis=0)
    pay[...] = jnp.broadcast_to(tile[None], pay.shape)
    for j in range(pay.shape[0]):
        for i in range(3):
            pay[j, 4 + i : 5 + i, :] = sums[i, j // 2 : j // 2 + 1, lanes(j % 2)]


def back_kernel(
    len_ref, half_ref, ends, got, params, stats, conv_a, conv_b, grad_scaled, value_a, value_b, sig_a, sig_b,
    taps, left, out_rows,
    own_pre, shift_grad, gain_grad, pay, work, grad_pre,
):
    rows, channels = conv_a.shape
    width = 2 * channels
    peers, rows_dev, _ = pay.shape
    total = params[2:3]
    sums = tree_sum(got[...])
    mean, inv_std = stats[0:1], stats[1:2]
    slices = []
    for h in range(channels // LANES):
        cols = lanes(h)
        s, q = sums[h : h + 1], sums[2 + h : 3 + h]
        shift_grad[:, cols] = s
        gain_grad[:, cols] = q
        scale = params[0:1, cols] * inv_std[:, cols]
        s, q = s / total[:, cols], q / total[:, cols]
        for part, (conv_out, value, sig) in enumerate(((conv_a, value_a, sig_a), (conv_b, value_b, sig_b))):
            masks = own_masks(len_ref, rows) if part == 0 else row_masks(ends[0:1], ends[1:2], rows)
            first, live = masks
            span = slice(part * rows, (part + 1) * rows)
            norm = (conv_out[:, cols] - mean[:, cols]) * inv_std[:, cols]
            grad = scale * (grad_scaled[span, cols] - s - norm * q)
            embed(work, h, jnp.where(live, grad, 0.0), first)
            glu = jnp.where(live, conv(work, h, taps, rows, first, -1), 0.0)
            v, g = value[:, cols], sig[:, cols]
            grad_pre[span, cols] = (glu * g).astype(BF16)
            grad_pre[span, channels + h * LANES : channels + (h + 1) * LANES] = (
                glu * v * g * (1.0 - g)
            ).astype(BF16)
        own, ones, cv = sums[4:5], sums[5:6], sums[6:7]
        slices.append(scale * (own - s * ones - q * inv_std[:, cols] * (cv - mean[:, cols] * ones)))
    own_pre[...] = grad_pre[:rows]
    which = jnp.full((1, LANES), half_ref[0], jnp.int32)
    depth = jnp.where(which == 0, slices[0], slices[1]).astype(BF16)
    total = jnp.dot(left[...], grad_pre[...], preferred_element_type=F32)
    pay[:, :, :width] = total.reshape(peers, rows_dev, width).astype(BF16)
    pay[:, :, width : width + channels] = out_rows[...]
    pay[:, :, width + channels :] = jnp.broadcast_to(depth[None], (peers, rows_dev, LANES))


def frame_kernel(mp_ref, grad_pre, proj, own, one, two, three):
    width = own.shape[1]
    groups = proj.shape[0] // width
    for d, out in enumerate((own, one, two, three)):
        at = pl.multiple_of(lax.rem(mp_ref[0] + d, groups) * width, width)
        term = lax.dot_general(grad_pre[...], proj[pl.ds(at, width), :], NT, preferred_element_type=F32)
        out[...] = term.astype(BF16)


def rows_kernel(left, right, out):
    out[...] = jnp.dot(left[...], right[...], preferred_element_type=F32).astype(BF16)


def last_kernel(got, in_rows, out_rows, depth):
    more = out_rows.shape[1]
    width = 2 * more
    for g in range(2):
        total = jnp.zeros((in_rows.shape[0], more), F32)
        for j in range(got.shape[0]):
            total = total + got[j, :, g * more : (g + 1) * more].astype(F32)
        in_rows[:, g, :] = total
    total = jnp.zeros((in_rows.shape[0], more), F32)
    for j in range(got.shape[0]):
        total = total + got[j, :, width : width + more].astype(F32)
    out_rows[...] = total
    for j in range(2 * depth.shape[0]):
        depth[j // 2 : j // 2 + 1, lanes(j % 2)] = got[j, 0:1, width + more :].astype(F32)


def core_rows(x, other, core):
    frames, width = x.shape
    halves = []
    for part in (x, other):
        rows = part.T.reshape(width // 16, 2, 8, frames)
        halves.append(lax.dynamic_index_in_dim(rows, core, 1, keepdims=False).reshape(width // 2, frames))
    return jnp.concatenate(halves, axis=1)


def swap_cores(x):
    return lax.ppermute(x, "core", [(0, 1), (1, 0)])


def after(x, y):
    return lax.optimization_barrier((x, y))[0]


def shards(frames, proj_in, taps, bn_gain, bn_shift, proj_out, grad_out, counts, lengths):
    rows, width = frames.shape
    channels = proj_in.shape[2]
    count = taps.shape[0]
    halves = channels // LANES
    buf_rows = rows + 3 * PAD
    peers = lax.axis_size(DP)
    chips = lax.axis_size(YZ)
    groups = lax.axis_size("mp")
    rows_dev = width // peers
    core = lax.axis_index("core")
    chip = lax.axis_index(YZ)
    mp = lax.axis_index("mp")
    full = shape((rows, channels))
    buf_shape = (halves, buf_rows, LANES)
    tap_shape = (count + 1, channels)
    wide = pltpu.VMEM((rows, 2 * channels), F32)
    square = pltpu.VMEM((rows, channels), F32)
    work = pltpu.VMEM(buf_shape, F32)
    proj = proj_in.reshape(width, 2 * channels)
    counts_row = counts.reshape(1, -1)
    gain_row = bn_gain.reshape(1, channels)
    shift_row = bn_shift.reshape(1, channels)

    conv_a, buf_a, pay = call(
        forward_kernel,
        (full, shape(buf_shape), hbm_shape((peers, 2, channels))),
        [SM, VM, VM, VM],
        [wide],
        name="forward",
    )(lengths, frames, proj, taps)
    got = lax.all_to_all(pay, DP, 0, 0)

    spans = jnp.pad(lengths.astype(BF16), ((0, 15), (0, width - lengths.shape[1])))
    given = swap_cores(after(jnp.concatenate([frames, grad_out, spans], axis=0), pay))
    value_a, sig_a, hid_a, ones_a, conv_sum_a, params = call(
        side_kernel,
        (
            hbm_shape((rows, channels)),
            hbm_shape((rows, channels)),
            full,
            shape(tap_shape),
            shape(tap_shape),
            shape((8, channels)),
        ),
        [SM, HB, HB, HB, HB, VM, VM, HB, HB, HB],
        [wide, square, work],
        name="side",
    )(lengths, frames, proj, grad_out, proj_out, conv_a, buf_a, gain_row, shift_row, counts_row)
    value_b, sig_b, hid_b, ones_b, conv_sum_b, conv_b, buf_b, ends = call(
        mirror_kernel,
        (
            hbm_shape((rows, channels)),
            hbm_shape((rows, channels)),
            full,
            shape(tap_shape),
            shape(tap_shape),
            full,
            shape(buf_shape),
            shape((8, LANES)),
        ),
        [HB, HB, HB, HB],
        [wide, square, work],
        name="mirror",
    )(given, proj, proj_out, taps)

    hidden, grad_scaled, stats, pay = call(
        norm_kernel,
        (
            shape((2 * rows, channels), BF16),
            shape((2 * rows, channels)),
            shape((2, channels)),
            hbm_shape((chips, 8, LANES)),
        ),
        [SM] + [VM] * 13,
        [work, pltpu.VMEM((3,) + tap_shape, F32)],
        name="norm",
    )(lengths, ends, got, params, conv_a, conv_b, hid_a, hid_b, buf_a, buf_b, ones_a, ones_b, conv_sum_a, conv_sum_b)
    got = lax.all_to_all(pay, YZ, 0, 0)

    given = after(given, pay)
    left_in = core_rows(frames, given[:rows], core)
    left_out = core_rows(grad_out, given[rows : 2 * rows], core)
    (out_rows,) = call(rows_kernel, (shape((width // 2, channels), BF16),), [HB, VM], name="out_rows")(
        left_out, hidden
    )
    got, out_rows, left_in = lax.optimization_barrier((got, out_rows, left_in))
    out_rows = out_rows.reshape(chips, rows_dev, channels)

    half = (chip % 2).astype(jnp.int32).reshape(1)
    grad_pre, shift_grad, gain_grad, pay = call(
        back_kernel,
        (
            shape((rows, 2 * channels), BF16),
            hbm_shape((1, channels)),
            hbm_shape((1, channels)),
            hbm_shape((chips, rows_dev, 3 * channels + LANES), BF16),
        ),
        [SM, SM] + [VM] * 14,
        [work, pltpu.VMEM((2 * rows, 2 * channels), BF16)],
        name="back",
    )(
        lengths, half, ends, got, params, stats, conv_a, conv_b, grad_scaled, value_a, value_b, sig_a, sig_b,
        taps, left_in, out_rows,
    )
    got = lax.all_to_all(pay, YZ, 0, 0)

    term = shape((rows, width // groups), BF16)
    own, one, two, three = call(frame_kernel, (term,) * 4, [SM, VM, HB], name="frame")(
        mp.astype(jnp.int32).reshape(1), grad_pre, proj
    )

    frame_sum = own.astype(F32)
    for d, part in ((1, one), (2, two), (3, three)):
        part = lax.ppermute(after(part, pay), "mp", [(i, (i + d) % groups) for i in range(groups)])
        frame_sum = frame_sum + part.astype(F32)
    frame_grad = frame_sum.astype(BF16)

    in_grad, out_grad, depth_grad = call(
        last_kernel,
        (hbm_shape((rows_dev, 2, channels)), hbm_shape((rows_dev, channels)), hbm_shape((count, channels))),
        [VM],
        name="last",
    )(got)
    return (frame_grad, in_grad, out_grad, depth_grad, gain_grad.reshape(channels), shift_grad.reshape(channels))


def solution(mesh):
    grid = Mesh(mesh.devices.reshape(8, 8, 2, 4), ("y", "z", "core", "mp"))
    placed = (
        P(DP, None),
        P(None, None, "mp"),
        P(None, "mp"),
        P("mp"),
        P("mp"),
        P(None, "mp"),
        P(DP, None),
        P(),
        P(DP, None),
    )
    return jax.shard_map(
        shards,
        mesh=grid,
        in_specs=placed,
        out_specs=(
            P(DP, "mp"),
            P(DP, None, "mp"),
            P(DP, "mp"),
            P(None, "mp"),
            P("mp"),
            P("mp"),
        ),
        check_vma=False,
    )
```

```python
import jax
import jax.numpy as jnp
from jax import lax
from jax.experimental import pallas as pl
from jax.experimental.pallas import tpu as pltpu
from jax.sharding import Mesh, PartitionSpec as P


BLOCK = 128
DP = ("y", "z", "core")
YZ = ("y", "z")
LANES = 128
TAPS = 31
PAD = 16
F32 = jnp.float32
BF16 = jnp.bfloat16
VM = pl.BlockSpec(memory_space=pltpu.VMEM)
HB = pl.BlockSpec(memory_space=pltpu.VMEM)
AN = pl.BlockSpec(memory_space=pl.ANY)
SM = pl.BlockSpec(memory_space=pltpu.SMEM)
NT = (((1,), (1,)), ((), ()))


def call(body, outs, ins, scratch=()):
    kernel = pl.pallas_call(
        body, out_shape=outs, in_specs=ins, out_specs=tuple(VM for _ in outs), scratch_shapes=list(scratch)
    )

    def run(*args):
        held = [
            pltpu.with_memory_space_constraint(a, pltpu.VMEM) if spec is VM else a
            for a, spec in zip(args, ins)
        ]
        return kernel(*held)

    return run


def shape(dims, dtype=F32):
    return pltpu.VMEM(dims, dtype)


def hbm_shape(dims, dtype=F32):
    return jax.ShapeDtypeStruct(dims, dtype)


def tree_sum(x):
    while x.shape[0] > 1:
        half = x.shape[0] // 2
        x = x[:half] + x[half:]
    return x[0]


def lanes(h):
    return slice(h * LANES, (h + 1) * LANES)


def row_masks(split, end, rows):
    row = lax.broadcasted_iota(jnp.int32, (rows, LANES), 0).astype(F32)
    return row < split, row < end


def own_masks(len_ref, rows):
    split = len_ref[0, 0]
    return row_masks(split.astype(F32), (split + len_ref[0, 1]).astype(F32), rows)


def embed(buf, h, x, first):
    rows = x.shape[0]
    zero = jnp.zeros((PAD, LANES), F32)
    head = jnp.where(first, x, 0.0)
    tail = jnp.where(first, 0.0, x)
    buf[h, 0:PAD] = zero
    buf[h, PAD : 2 * PAD] = head[:PAD]
    buf[h, 2 * PAD : PAD + rows] = head[PAD:] + tail[: rows - PAD]
    buf[h, PAD + rows : 2 * PAD + rows] = tail[rows - PAD :]
    buf[h, 2 * PAD + rows : 3 * PAD + rows] = zero


def conv(buf, h, taps, rows, first, sign):
    count = taps.shape[0]
    radius = count // 2
    span = rows + PAD
    total = jnp.zeros((span, LANES), F32)
    for k in range(count):
        total = total + taps[k : k + 1, lanes(h)] * buf[h, pl.ds(PAD + sign * (k - radius), span), :]
    return jnp.where(first, total[:rows], total[PAD:])


def tap_sums(out, values, buf, h, count, rows):
    radius = count // 2
    span = rows + PAD
    for k in range(count):
        prod = values * buf[h, pl.ds(PAD + k - radius, span), :]
        out[k : k + 1, lanes(h)] = jnp.sum(prod, axis=0, keepdims=True)


def fetches(sources, targets, sems):
    copies = [pltpu.make_async_copy(a, b, sems.at[i]) for i, (a, b) in enumerate(zip(sources, targets))]
    for copy in copies:
        copy.start()
    return copies


def batch_norm(conv_out, mean, inv_std, params, cols):
    norm = (conv_out[:, cols] - mean[:, cols]) * inv_std[:, cols]
    scaled = norm * params[0:1, cols] + params[1:2, cols]
    return norm, scaled, jax.nn.sigmoid(scaled)


def swish_slope(scaled, s):
    return s * (1.0 + scaled * (1.0 - s))


def gated(pre, live, h, channels):
    value = pre[:, lanes(h)]
    sig = jax.nn.sigmoid(pre[:, channels + h * LANES : channels + (h + 1) * LANES])
    return value, sig, jnp.where(live, value * sig, 0.0).astype(BF16).astype(F32)


def forward_kernel(len_ref, frames, proj, taps, conv_out, buf, pay, pre):
    rows, channels = conv_out.shape
    first, live = own_masks(len_ref, rows)
    pre[...] = jnp.dot(frames[...], proj[...], preferred_element_type=F32)
    sums = []
    for h in range(channels // LANES):
        _, _, glu = gated(pre, live, h, channels)
        embed(buf, h, glu, first)
        out = jnp.where(live, conv(buf, h, taps, rows, first, 1), 0.0)
        conv_out[:, lanes(h)] = out
        sums.append(
            jnp.concatenate(
                [jnp.sum(out, axis=0, keepdims=True), jnp.sum(out * out, axis=0, keepdims=True)], axis=0
            )
        )
    both = jnp.concatenate(sums, axis=1)
    pay[...] = jnp.broadcast_to(both[None], pay.shape)


def known_sums(ones_sum, conv_sum, conv_out, buf, work, h, rows, first, live):
    count = TAPS
    embed(work, h, jnp.where(live, 1.0, 0.0), first)
    tap_sums(ones_sum, work[h, pl.ds(PAD, rows + PAD), :], buf, h, count, rows)
    embed(work, h, conv_out[:, lanes(h)], first)
    tap_sums(conv_sum, work[h, pl.ds(PAD, rows + PAD), :], buf, h, count, rows)
    ones_sum[count : count + 1, lanes(h)] = jnp.zeros((1, LANES), F32)
    conv_sum[count : count + 1, lanes(h)] = jnp.zeros((1, LANES), F32)


def side_kernel(
    len_ref, frames, proj, grad_out, proj_out, conv_out, buf, gain, shift, counts,
    value, sig, grad_hidden, ones_sum, conv_sum, params, pre, hid, work,
):
    rows, channels = conv_out.shape
    first, live = own_masks(len_ref, rows)
    pre[...] = jnp.dot(frames[...], proj[...], preferred_element_type=F32)
    hid[...] = jnp.dot(grad_out[...], proj_out[...], preferred_element_type=F32)
    for h in range(channels // LANES):
        cols = lanes(h)
        value[:, cols], sig[:, cols], _ = gated(pre, live, h, channels)
        grad_hidden[:, cols] = jnp.where(live, hid[:, cols], 0.0)
        known_sums(ones_sum, conv_sum, conv_out, buf, work, h, rows, first, live)
    total = jnp.sum(counts[...].astype(F32), axis=1, keepdims=True) * BLOCK
    params[0:1] = gain[...]
    params[1:2] = shift[...]
    params[2:3] = jnp.broadcast_to(total, (1, channels))
    params[3:] = jnp.zeros((5, channels), F32)


def mirror_kernel(
    given, proj, proj_out, taps,
    value, sig, grad_hidden, ones_sum, conv_sum, conv_out, buf, ends, pre, hid, work,
):
    rows, channels = conv_out.shape
    spans = given[2 * rows : 2 * rows + 16, :LANES].astype(F32)[0:1]
    split = spans[:, 0:1]
    end = split + spans[:, 1:2]
    ends[0:1] = jnp.broadcast_to(split, (1, LANES))
    ends[1:2] = jnp.broadcast_to(end, (1, LANES))
    ends[2:] = jnp.zeros((6, LANES), F32)
    first, live = row_masks(ends[0:1], ends[1:2], rows)
    pre[...] = jnp.dot(given[:rows], proj[...], preferred_element_type=F32)
    hid[...] = jnp.dot(given[rows : 2 * rows], proj_out[...], preferred_element_type=F32)
    for h in range(channels // LANES):
        cols = lanes(h)
        value[:, cols], sig[:, cols], glu = gated(pre, live, h, channels)
        embed(buf, h, glu, first)
        conv_out[:, cols] = jnp.where(live, conv(buf, h, taps, rows, first, 1), 0.0)
        grad_hidden[:, cols] = jnp.where(live, hid[:, cols], 0.0)
        known_sums(ones_sum, conv_sum, conv_out, buf, work, h, rows, first, live)


def norm_kernel(
    len_ref, ends, got, params, conv_a, conv_b, hid_a, hid_b, buf_a, buf_b,
    ones_a, ones_b, conv_sum_a, conv_sum_b,
    hidden, stats, pay, work, sums, hids, bufs, sems,
):
    rows, channels = conv_a.shape
    count = TAPS
    copies = fetches((hid_a, hid_b, buf_a, buf_b), (hids.at[0], hids.at[1], bufs.at[0], bufs.at[1]), sems)
    total = params[2:3]
    found = tree_sum(got[...])
    mean = found[0:1] / total
    inv_std = lax.rsqrt(found[1:2] / total - mean * mean + 1e-05)
    stats[0:1] = mean
    stats[1:2] = inv_std
    sums[1] = ones_a[...] + ones_b[...]
    sums[2] = conv_sum_a[...] + conv_sum_b[...]
    for copy in copies:
        copy.wait()
    heads = []
    for h in range(channels // LANES):
        cols = lanes(h)
        head = []
        for part, conv_out in enumerate((conv_a, conv_b)):
            masks = own_masks(len_ref, rows) if part == 0 else row_masks(ends[0:1], ends[1:2], rows)
            first, live = masks
            norm, scaled, s = batch_norm(conv_out, mean, inv_std, params, cols)
            hidden[part * rows : (part + 1) * rows, cols] = jnp.where(live, scaled * s, 0.0).astype(BF16)
            grad = hids[part, :, cols] * swish_slope(scaled, s)
            head.append((jnp.sum(grad, axis=0, keepdims=True), jnp.sum(grad * norm, axis=0, keepdims=True)))
            embed(work, h, grad, first)
            out = sums.at[0] if part == 0 else sums.at[3]
            tap_sums(out, work[h, pl.ds(PAD, rows + PAD), :], bufs.at[part], h, count, rows)
            out[count : count + 1, cols] = jnp.zeros((1, LANES), F32)
        heads.append([a + b for a, b in zip(*head)])
    sums[0] = sums[0] + sums[3]
    (s0, q0), (s1, q1) = heads
    tile = jnp.concatenate([s0, s1, q0, q1, jnp.zeros((4, LANES), F32)], axis=0)
    pay[...] = jnp.broadcast_to(tile[None], pay.shape)
    for j in range(pay.shape[0]):
        for i in range(3):
            pay[j, 4 + i : 5 + i, :] = sums[i, j // 2 : j // 2 + 1, lanes(j % 2)]


def back_kernel(
    len_ref, half_ref, ends, got, params, stats, conv_a, conv_b, taps,
    hid_a, hid_b, value_a, value_b, sig_a, sig_b, left_in, rows_in,
    own_pre, shift_grad, gain_grad, pay, work, grad_pre, hids, values, sigs, left, out_rows, sems,
):
    rows, channels = conv_a.shape
    width = 2 * channels
    peers, rows_dev, _ = pay.shape
    copies = fetches(
        (hid_a, hid_b, value_a, value_b, sig_a, sig_b, left_in, rows_in),
        (hids.at[0], hids.at[1], values.at[0], values.at[1], sigs.at[0], sigs.at[1], left, out_rows),
        sems,
    )
    total = params[2:3]
    sums = tree_sum(got[...])
    mean, inv_std = stats[0:1], stats[1:2]
    copies[0].wait()
    copies[1].wait()
    slices = []
    for h in range(channels // LANES):
        cols = lanes(h)
        s, q = sums[h : h + 1], sums[2 + h : 3 + h]
        shift_grad[:, cols] = s
        gain_grad[:, cols] = q
        scale = params[0:1, cols] * inv_std[:, cols]
        s, q = s / total[:, cols], q / total[:, cols]
        for part, conv_out in enumerate((conv_a, conv_b)):
            masks = own_masks(len_ref, rows) if part == 0 else row_masks(ends[0:1], ends[1:2], rows)
            first, live = masks
            span = slice(part * rows, (part + 1) * rows)
            norm, scaled, swish = batch_norm(conv_out, mean, inv_std, params, cols)
            grad = scale * (hids[part, :, cols] * swish_slope(scaled, swish) - s - norm * q)
            embed(work, h, jnp.where(live, grad, 0.0), first)
            glu = jnp.where(live, conv(work, h, taps, rows, first, -1), 0.0)
            if h == 0:
                copies[2 + part].wait()
                copies[4 + part].wait()
            v, g = values[part, :, cols], sigs[part, :, cols]
            grad_pre[span, cols] = (glu * g).astype(BF16)
            grad_pre[span, channels + h * LANES : channels + (h + 1) * LANES] = (
                glu * v * g * (1.0 - g)
            ).astype(BF16)
        own, ones, cv = sums[4:5], sums[5:6], sums[6:7]
        slices.append(scale * (own - s * ones - q * inv_std[:, cols] * (cv - mean[:, cols] * ones)))
    own_pre[...] = grad_pre[:rows]
    which = jnp.full((1, LANES), half_ref[0], jnp.int32)
    depth = jnp.where(which == 0, slices[0], slices[1]).astype(BF16)
    copies[6].wait()
    copies[7].wait()
    total = jnp.dot(left[...], grad_pre[...], preferred_element_type=F32)
    pay[:, :, :width] = total.reshape(peers, rows_dev, width).astype(BF16)
    pay[:, :, width : width + channels] = out_rows[...]
    pay[:, :, width + channels :] = jnp.broadcast_to(depth[None], (peers, rows_dev, LANES))


def frame_kernel(mp_ref, grad_pre, proj, own, one, two, three):
    width = own.shape[1]
    groups = proj.shape[0] // width
    for d, out in enumerate((own, one, two, three)):
        at = pl.multiple_of(lax.rem(mp_ref[0] + d, groups) * width, width)
        term = lax.dot_general(grad_pre[...], proj[pl.ds(at, width), :], NT, preferred_element_type=F32)
        out[...] = term.astype(BF16)


def rows_kernel(left, right, out):
    out[...] = jnp.dot(left[...], right[...], preferred_element_type=F32).astype(BF16)


def last_kernel(got, in_rows, out_rows, depth):
    more = out_rows.shape[1]
    width = 2 * more
    for g in range(2):
        total = jnp.zeros((in_rows.shape[0], more), F32)
        for j in range(got.shape[0]):
            total = total + got[j, :, g * more : (g + 1) * more].astype(F32)
        in_rows[:, g, :] = total
    total = jnp.zeros((in_rows.shape[0], more), F32)
    for j in range(got.shape[0]):
        total = total + got[j, :, width : width + more].astype(F32)
    out_rows[...] = total
    for j in range(2 * depth.shape[0]):
        depth[j // 2 : j // 2 + 1, lanes(j % 2)] = got[j, 0:1, width + more :].astype(F32)


def core_rows(x, other, core):
    frames, width = x.shape
    halves = []
    for part in (x, other):
        rows = part.T.reshape(width // 16, 2, 8, frames)
        halves.append(lax.dynamic_index_in_dim(rows, core, 1, keepdims=False).reshape(width // 2, frames))
    return jnp.concatenate(halves, axis=1)


def swap_cores(x):
    return lax.ppermute(x, "core", [(0, 1), (1, 0)])


def after(x, y):
    return lax.optimization_barrier((x, y))[0]


def shards(frames, proj_in, taps, bn_gain, bn_shift, proj_out, grad_out, counts, lengths):
    rows, width = frames.shape
    channels = proj_in.shape[2]
    count = taps.shape[0]
    halves = channels // LANES
    buf_rows = rows + 3 * PAD
    peers = lax.axis_size(DP)
    chips = lax.axis_size(YZ)
    groups = lax.axis_size("mp")
    rows_dev = width // peers
    core = lax.axis_index("core")
    chip = lax.axis_index(YZ)
    mp = lax.axis_index("mp")
    full = shape((rows, channels))
    buf_shape = (halves, buf_rows, LANES)
    tap_shape = (count + 1, channels)
    wide = pltpu.VMEM((rows, 2 * channels), F32)
    square = pltpu.VMEM((rows, channels), F32)
    work = pltpu.VMEM(buf_shape, F32)
    proj = proj_in.reshape(width, 2 * channels)
    counts_row = counts.reshape(1, -1)
    gain_row = bn_gain.reshape(1, channels)
    shift_row = bn_shift.reshape(1, channels)

    conv_a, buf_a, pay = call(
        forward_kernel, (full, shape(buf_shape), hbm_shape((peers, 2, channels))), [SM, VM, VM, VM], [wide]
    )(lengths, frames, proj, taps)
    got = lax.all_to_all(pay, DP, 0, 0)

    spans = jnp.pad(lengths.astype(BF16), ((0, 15), (0, width - lengths.shape[1])))
    given = after(jnp.concatenate([frames, grad_out, spans], axis=0), pay)
    given = swap_cores(given)
    value_a, sig_a, hid_a, ones_a, conv_sum_a, params = call(
        side_kernel,
        (
            hbm_shape((rows, channels)),
            hbm_shape((rows, channels)),
            hbm_shape((rows, channels)),
            shape(tap_shape),
            shape(tap_shape),
            shape((8, channels)),
        ),
        [SM, HB, HB, HB, HB, VM, VM, HB, HB, HB],
        [wide, square, work],
    )(lengths, frames, proj, grad_out, proj_out, conv_a, buf_a, gain_row, shift_row, counts_row)
    value_b, sig_b, hid_b, ones_b, conv_sum_b, conv_b, buf_b, ends = call(
        mirror_kernel,
        (
            hbm_shape((rows, channels)),
            hbm_shape((rows, channels)),
            hbm_shape((rows, channels)),
            shape(tap_shape),
            shape(tap_shape),
            full,
            hbm_shape(buf_shape),
            shape((8, LANES)),
        ),
        [HB, HB, HB, HB],
        [wide, square, work],
    )(given, proj, proj_out, taps)

    hidden, stats, pay = call(
        norm_kernel,
        (
            shape((2 * rows, channels), BF16),
            shape((2, channels)),
            hbm_shape((chips, 8, LANES)),
        ),
        [SM] + [VM] * 5 + [AN] * 4 + [VM] * 4,
        [
            work,
            pltpu.VMEM((4,) + tap_shape, F32),
            pltpu.VMEM((2, rows, channels), F32),
            pltpu.VMEM((2,) + buf_shape, F32),
            pltpu.SemaphoreType.DMA((4,)),
        ],
    )(lengths, ends, got, params, conv_a, conv_b, hid_a, hid_b, buf_a, buf_b, ones_a, ones_b, conv_sum_a, conv_sum_b)
    got = lax.all_to_all(pay, YZ, 0, 0)

    given, frames, grad_out, _ = lax.optimization_barrier((given, frames, grad_out, pay))
    left_in = core_rows(frames, given[:rows], core)
    left_out = core_rows(grad_out, given[rows : 2 * rows], core)
    (out_rows,) = call(rows_kernel, (hbm_shape((width // 2, channels), BF16),), [HB, VM])(left_out, hidden)
    got, out_rows, left_in = lax.optimization_barrier((got, out_rows, left_in))
    out_rows = out_rows.reshape(chips, rows_dev, channels)

    half = (chip % 2).astype(jnp.int32).reshape(1)
    grad_pre, shift_grad, gain_grad, pay = call(
        back_kernel,
        (
            shape((rows, 2 * channels), BF16),
            hbm_shape((1, channels)),
            hbm_shape((1, channels)),
            hbm_shape((chips, rows_dev, 3 * channels + LANES), BF16),
        ),
        [SM, SM] + [VM] * 7 + [AN] * 8,
        [
            work,
            pltpu.VMEM((2 * rows, 2 * channels), BF16),
            pltpu.VMEM((2, rows, channels), F32),
            pltpu.VMEM((2, rows, channels), F32),
            pltpu.VMEM((2, rows, channels), F32),
            pltpu.VMEM((width // 2, 2 * rows), BF16),
            pltpu.VMEM((chips, rows_dev, channels), BF16),
            pltpu.SemaphoreType.DMA((8,)),
        ],
    )(
        lengths, half, ends, got, params, stats, conv_a, conv_b, taps,
        hid_a, hid_b, value_a, value_b, sig_a, sig_b, left_in, out_rows,
    )
    got = lax.all_to_all(pay, YZ, 0, 0)

    term = shape((rows, width // groups), BF16)
    own, one, two, three = call(frame_kernel, (term,) * 4, [SM, VM, HB])(
        mp.astype(jnp.int32).reshape(1), grad_pre, proj
    )

    frame_sum = own.astype(F32)
    for d, part in ((1, one), (2, two), (3, three)):
        part = lax.ppermute(after(part, pay), "mp", [(i, (i + d) % groups) for i in range(groups)])
        frame_sum = frame_sum + part.astype(F32)
    frame_grad = frame_sum.astype(BF16)

    in_grad, out_grad, depth_grad = call(
        last_kernel,
        (hbm_shape((rows_dev, 2, channels)), hbm_shape((rows_dev, channels)), hbm_shape((count, channels))),
        [VM],
    )(got)
    return (frame_grad, in_grad, out_grad, depth_grad, gain_grad.reshape(channels), shift_grad.reshape(channels))


def solution(mesh):
    grid = Mesh(mesh.devices.reshape(8, 8, 2, 4), ("y", "z", "core", "mp"))
    placed = (
        P(DP, None),
        P(None, None, "mp"),
        P(None, "mp"),
        P("mp"),
        P("mp"),
        P(None, "mp"),
        P(DP, None),
        P(),
        P(DP, None),
    )
    return jax.shard_map(
        shards,
        mesh=grid,
        in_specs=placed,
        out_specs=(
            P(DP, "mp"),
            P(DP, None, "mp"),
            P(DP, "mp"),
            P(None, "mp"),
            P("mp"),
            P("mp"),
        ),
        check_vma=False,
    )
```

```python
import jax
import jax.numpy as jnp
from jax import lax
from jax.experimental import pallas as pl
from jax.experimental.pallas import tpu as pltpu
from jax.sharding import Mesh, PartitionSpec as P


BLOCK = 128
DP = ("y", "z", "core")
YZ = ("y", "z")
LANES = 128
TAPS = 31
PAD = 16
F32 = jnp.float32
BF16 = jnp.bfloat16
VM = pl.BlockSpec(memory_space=pltpu.VMEM)
HB = pl.BlockSpec(memory_space=pltpu.VMEM)
AN = pl.BlockSpec(memory_space=pl.ANY)
SM = pl.BlockSpec(memory_space=pltpu.SMEM)
NT = (((1,), (1,)), ((), ()))


def call(body, outs, ins, scratch=()):
    kernel = pl.pallas_call(
        body, out_shape=outs, in_specs=ins, out_specs=tuple(VM for _ in outs), scratch_shapes=list(scratch)
    )

    def run(*args):
        held = [
            pltpu.with_memory_space_constraint(a, pltpu.VMEM) if spec is VM else a
            for a, spec in zip(args, ins)
        ]
        return kernel(*held)

    return run


def shape(dims, dtype=F32):
    return pltpu.VMEM(dims, dtype)


def hbm_shape(dims, dtype=F32):
    return jax.ShapeDtypeStruct(dims, dtype)


def tree_sum(x):
    while x.shape[0] > 1:
        half = x.shape[0] // 2
        x = x[:half] + x[half:]
    return x[0]


def lanes(h):
    return slice(h * LANES, (h + 1) * LANES)


def row_masks(split, end, rows):
    row = lax.broadcasted_iota(jnp.int32, (rows, LANES), 0).astype(F32)
    return row < split, row < end


def own_masks(len_ref, rows):
    split = len_ref[0, 0]
    return row_masks(split.astype(F32), (split + len_ref[0, 1]).astype(F32), rows)


def embed(buf, h, x, first):
    rows = x.shape[0]
    zero = jnp.zeros((PAD, LANES), F32)
    head = jnp.where(first, x, 0.0)
    tail = jnp.where(first, 0.0, x)
    buf[h, 0:PAD] = zero
    buf[h, PAD : 2 * PAD] = head[:PAD]
    buf[h, 2 * PAD : PAD + rows] = head[PAD:] + tail[: rows - PAD]
    buf[h, PAD + rows : 2 * PAD + rows] = tail[rows - PAD :]
    buf[h, 2 * PAD + rows : 3 * PAD + rows] = zero


def conv(buf, h, taps, rows, first, sign):
    count = taps.shape[0]
    radius = count // 2
    span = rows + PAD
    total = jnp.zeros((span, LANES), F32)
    for k in range(count):
        total = total + taps[k : k + 1, lanes(h)] * buf[h, pl.ds(PAD + sign * (k - radius), span), :]
    return jnp.where(first, total[:rows], total[PAD:])


def tap_sums(out, values, buf, h, count, rows):
    radius = count // 2
    span = rows + PAD
    for k in range(count):
        prod = values * buf[h, pl.ds(PAD + k - radius, span), :]
        out[k : k + 1, lanes(h)] = jnp.sum(prod, axis=0, keepdims=True)


def fetches(sources, targets, sems):
    copies = [pltpu.make_async_copy(a, b, sems.at[i]) for i, (a, b) in enumerate(zip(sources, targets))]
    for copy in copies:
        copy.start()
    return copies


def batch_norm(conv_out, mean, inv_std, params, cols):
    norm = (conv_out[:, cols] - mean[:, cols]) * inv_std[:, cols]
    scaled = norm * params[0:1, cols] + params[1:2, cols]
    return norm, scaled, jax.nn.sigmoid(scaled)


def swish_slope(scaled, s):
    return s * (1.0 + scaled * (1.0 - s))


def gated(pre, live, h, channels):
    value = pre[:, lanes(h)]
    sig = jax.nn.sigmoid(pre[:, channels + h * LANES : channels + (h + 1) * LANES])
    return value, sig, jnp.where(live, value * sig, 0.0).astype(BF16).astype(F32)


def forward_kernel(len_ref, frames, proj, taps, conv_out, buf, pay, pre):
    rows, channels = conv_out.shape
    first, live = own_masks(len_ref, rows)
    pre[...] = jnp.dot(frames[...], proj[...], preferred_element_type=F32)
    sums = []
    for h in range(channels // LANES):
        _, _, glu = gated(pre, live, h, channels)
        embed(buf, h, glu, first)
        out = jnp.where(live, conv(buf, h, taps, rows, first, 1), 0.0)
        conv_out[:, lanes(h)] = out
        sums.append(
            jnp.concatenate(
                [jnp.sum(out, axis=0, keepdims=True), jnp.sum(out * out, axis=0, keepdims=True)], axis=0
            )
        )
    both = jnp.concatenate(sums, axis=1)
    pay[...] = jnp.broadcast_to(both[None], pay.shape)


def live_taps(split, end, rows):
    dims = (TAPS + 1, rows + 3 * PAD)
    tap = lax.broadcasted_iota(jnp.int32, dims, 0)
    at = lax.broadcasted_iota(jnp.int32, dims, 1) - tap + TAPS // 2
    one = (at >= PAD) & (at < PAD + split)
    two = (at >= 2 * PAD + split) & (at < 2 * PAD + end)
    return jnp.where(one | two, 1.0, 0.0).astype(BF16)


def side_kernel(
    len_ref, frames, proj, grad_out, proj_out, conv_out, buf, gain, shift, counts,
    value, sig, grad_hidden, ones_sum, conv_sum, params, pre, hid, work,
):
    rows, channels = conv_out.shape
    first, live = own_masks(len_ref, rows)
    marks = live_taps(len_ref[0, 0], len_ref[0, 0] + len_ref[0, 1], rows)
    pre[...] = jnp.dot(frames[...], proj[...], preferred_element_type=F32)
    hid[...] = jnp.dot(grad_out[...], proj_out[...], preferred_element_type=F32)
    for h in range(channels // LANES):
        cols = lanes(h)
        value[:, cols], sig[:, cols], _ = gated(pre, live, h, channels)
        grad_hidden[:, cols] = jnp.where(live, hid[:, cols], 0.0)
        ones_sum[:, cols] = jnp.dot(marks, buf[h].astype(BF16), preferred_element_type=F32)
        embed(work, h, conv_out[:, cols], first)
        tap_sums(conv_sum, work[h, pl.ds(PAD, rows + PAD), :], buf, h, TAPS, rows)
        conv_sum[TAPS : TAPS + 1, cols] = jnp.zeros((1, LANES), F32)
    total = jnp.sum(counts[...].astype(F32), axis=1, keepdims=True) * BLOCK
    params[0:1] = gain[...]
    params[1:2] = shift[...]
    params[2:3] = jnp.broadcast_to(total, (1, channels))
    params[3:] = jnp.zeros((5, channels), F32)


def mirror_kernel(
    given, proj, proj_out, taps, stats, params,
    value, sig, grad_hidden, conv_out, hidden, ends, pre, hid, buf,
):
    rows, channels = conv_out.shape
    spans = given[2 * rows : 2 * rows + 16, :LANES].astype(F32)[0:1]
    split = spans[:, 0:1]
    end = split + spans[:, 1:2]
    ends[0:1] = jnp.broadcast_to(split, (1, LANES))
    ends[1:2] = jnp.broadcast_to(end, (1, LANES))
    ends[2:] = jnp.zeros((6, LANES), F32)
    first, live = row_masks(ends[0:1], ends[1:2], rows)
    mean, inv_std = stats[0:1], stats[1:2]
    pre[...] = jnp.dot(given[:rows], proj[...], preferred_element_type=F32)
    hid[...] = jnp.dot(given[rows : 2 * rows], proj_out[...], preferred_element_type=F32)
    for h in range(channels // LANES):
        cols = lanes(h)
        value[:, cols], sig[:, cols], glu = gated(pre, live, h, channels)
        embed(buf, h, glu, first)
        conv_out[:, cols] = jnp.where(live, conv(buf, h, taps, rows, first, 1), 0.0)
        grad_hidden[:, cols] = jnp.where(live, hid[:, cols], 0.0)
        _, scaled, s = batch_norm(conv_out, mean, inv_std, params, cols)
        hidden[:, cols] = jnp.where(live, scaled * s, 0.0).astype(BF16)


def norm_kernel(
    len_ref, got, params, conv_out, grad_hidden, buf, ones_sum, conv_sum,
    hidden, stats, sums, work,
):
    rows, channels = conv_out.shape
    count = TAPS
    first, live = own_masks(len_ref, rows)
    total = params[2:3]
    found = tree_sum(got[...])
    mean = found[0:1] / total
    inv_std = lax.rsqrt(found[1:2] / total - mean * mean + 1e-05)
    stats[0:1] = mean
    stats[1:2] = inv_std
    base = 3 * (count + 1)
    sums[count + 1 : 2 * (count + 1)] = ones_sum[...]
    sums[2 * (count + 1) : base] = conv_sum[...]
    sums[base + 2 :] = jnp.zeros((6, channels), F32)
    for h in range(channels // LANES):
        cols = lanes(h)
        norm, scaled, s = batch_norm(conv_out, mean, inv_std, params, cols)
        hidden[:, cols] = jnp.where(live, scaled * s, 0.0).astype(BF16)
        grad = grad_hidden[:, cols] * swish_slope(scaled, s)
        sums[base : base + 1, cols] = jnp.sum(grad, axis=0, keepdims=True)
        sums[base + 1 : base + 2, cols] = jnp.sum(grad * norm, axis=0, keepdims=True)
        embed(work, h, grad, first)
        tap_sums(sums, work[h, pl.ds(PAD, rows + PAD), :], buf, h, count, rows)
        sums[count : count + 1, cols] = jnp.zeros((1, LANES), F32)


def spread_kernel(own, other, pay, sums):
    sums[...] = own[...] + other[...]
    count = pay.shape[0] // 2
    base = 3 * count
    tile = jnp.concatenate(
        [sums[base + i : base + i + 1, lanes(h)] for i in range(2) for h in range(2)]
        + [jnp.zeros((4, LANES), F32)],
        axis=0,
    )
    pay[...] = jnp.broadcast_to(tile[None], pay.shape)
    for j in range(pay.shape[0]):
        for i in range(3):
            at = i * count + j // 2
            pay[j, 4 + i : 5 + i, :] = sums[at : at + 1, lanes(j % 2)]


def back_kernel(
    len_ref, half_ref, ends, got, params, stats, conv_a, conv_b, taps,
    hid_a, hid_b, value_a, value_b, sig_a, sig_b, left_a, left_b, rows_in,
    own_pre, shift_grad, gain_grad, pay, work, grad_pre, hids, values, sigs, left, out_rows, sems,
):
    rows, channels = conv_a.shape
    width = 2 * channels
    peers, rows_dev, _ = pay.shape
    copies = fetches(
        (hid_a, hid_b, value_a, value_b, sig_a, sig_b, left_a, left_b, rows_in),
        (
            hids.at[0], hids.at[1], values.at[0], values.at[1], sigs.at[0], sigs.at[1],
            left.at[0], left.at[1], out_rows,
        ),
        sems,
    )
    total = params[2:3]
    sums = tree_sum(got[...])
    mean, inv_std = stats[0:1], stats[1:2]
    copies[0].wait()
    copies[1].wait()
    slices = []
    for h in range(channels // LANES):
        cols = lanes(h)
        s, q = sums[h : h + 1], sums[2 + h : 3 + h]
        shift_grad[:, cols] = s
        gain_grad[:, cols] = q
        scale = params[0:1, cols] * inv_std[:, cols]
        s, q = s / total[:, cols], q / total[:, cols]
        for part, conv_out in enumerate((conv_a, conv_b)):
            masks = own_masks(len_ref, rows) if part == 0 else row_masks(ends[0:1], ends[1:2], rows)
            first, live = masks
            span = slice(part * rows, (part + 1) * rows)
            norm, scaled, swish = batch_norm(conv_out, mean, inv_std, params, cols)
            grad = scale * (hids[part, :, cols] * swish_slope(scaled, swish) - s - norm * q)
            embed(work, h, jnp.where(live, grad, 0.0), first)
            glu = jnp.where(live, conv(work, h, taps, rows, first, -1), 0.0)
            if h == 0:
                copies[2 + part].wait()
                copies[4 + part].wait()
            v, g = values[part, :, cols], sigs[part, :, cols]
            grad_pre[span, cols] = (glu * g).astype(BF16)
            grad_pre[span, channels + h * LANES : channels + (h + 1) * LANES] = (
                glu * v * g * (1.0 - g)
            ).astype(BF16)
        own, ones, cv = sums[4:5], sums[5:6], sums[6:7]
        slices.append(scale * (own - s * ones - q * inv_std[:, cols] * (cv - mean[:, cols] * ones)))
    own_pre[...] = grad_pre[:rows]
    which = jnp.full((1, LANES), half_ref[0], jnp.int32)
    depth = jnp.where(which == 0, slices[0], slices[1]).astype(BF16)
    for copy in copies[6:]:
        copy.wait()
    total = jnp.dot(left[0], grad_pre[:rows], preferred_element_type=F32)
    total = total + jnp.dot(left[1], grad_pre[rows:], preferred_element_type=F32)
    pay[:, :, :width] = total.reshape(peers, rows_dev, width).astype(BF16)
    pay[:, :, width : width + channels] = out_rows[...]
    pay[:, :, width + channels :] = jnp.broadcast_to(depth[None], (peers, rows_dev, LANES))


def frame_kernel(mp_ref, grad_pre, proj, own, one, two, three):
    width = own.shape[1]
    groups = proj.shape[0] // width
    for d, out in enumerate((own, one, two, three)):
        at = pl.multiple_of(lax.rem(mp_ref[0] + d, groups) * width, width)
        term = lax.dot_general(grad_pre[...], proj[pl.ds(at, width), :], NT, preferred_element_type=F32)
        out[...] = term.astype(BF16)


def rows_kernel(left_a, left_b, right_a, right_b, out):
    total = jnp.dot(left_a[...], right_a[...], preferred_element_type=F32)
    total = total + jnp.dot(left_b[...], right_b[...], preferred_element_type=F32)
    out[...] = total.astype(BF16)


def last_kernel(got, in_rows, out_rows, depth):
    more = out_rows.shape[1]
    width = 2 * more
    for g in range(2):
        total = jnp.zeros((in_rows.shape[0], more), F32)
        for j in range(got.shape[0]):
            total = total + got[j, :, g * more : (g + 1) * more].astype(F32)
        in_rows[:, g, :] = total
    total = jnp.zeros((in_rows.shape[0], more), F32)
    for j in range(got.shape[0]):
        total = total + got[j, :, width : width + more].astype(F32)
    out_rows[...] = total
    for j in range(2 * depth.shape[0]):
        depth[j // 2 : j // 2 + 1, lanes(j % 2)] = got[j, 0:1, width + more :].astype(F32)


def core_rows(x, core):
    frames, width = x.shape
    rows = x.T.reshape(width // 16, 2, 8, frames)
    return lax.dynamic_index_in_dim(rows, core, 1, keepdims=False).reshape(width // 2, frames)


def swap_cores(x):
    return lax.ppermute(x, "core", [(0, 1), (1, 0)])


def after(x, y):
    return lax.optimization_barrier((x, y))[0]


def shards(frames, proj_in, taps, bn_gain, bn_shift, proj_out, grad_out, counts, lengths):
    rows, width = frames.shape
    channels = proj_in.shape[2]
    count = taps.shape[0]
    halves = channels // LANES
    buf_rows = rows + 3 * PAD
    peers = lax.axis_size(DP)
    chips = lax.axis_size(YZ)
    groups = lax.axis_size("mp")
    rows_dev = width // peers
    core = lax.axis_index("core")
    chip = lax.axis_index(YZ)
    mp = lax.axis_index("mp")
    full = shape((rows, channels))
    buf_shape = (halves, buf_rows, LANES)
    tap_shape = (count + 1, channels)
    wide = pltpu.VMEM((rows, 2 * channels), F32)
    square = pltpu.VMEM((rows, channels), F32)
    work = pltpu.VMEM(buf_shape, F32)
    proj = proj_in.reshape(width, 2 * channels)
    counts_row = counts.reshape(1, -1)
    gain_row = bn_gain.reshape(1, channels)
    shift_row = bn_shift.reshape(1, channels)

    conv_a, buf_a, pay = call(
        forward_kernel, (full, shape(buf_shape), hbm_shape((peers, 2, channels))), [SM, VM, VM, VM], [wide]
    )(lengths, frames, proj, taps)
    got = lax.all_to_all(pay, DP, 0, 0)

    spans = jnp.pad(lengths.astype(BF16), ((0, 15), (0, width - lengths.shape[1])))
    given = after(jnp.concatenate([frames, grad_out, spans], axis=0), pay)
    given = swap_cores(given)
    value_a, sig_a, hid_a, ones_a, conv_sum_a, params = call(
        side_kernel,
        (
            hbm_shape((rows, channels)),
            hbm_shape((rows, channels)),
            full,
            shape(tap_shape),
            shape(tap_shape),
            shape((8, channels)),
        ),
        [SM, HB, HB, HB, HB, VM, VM, HB, HB, HB],
        [wide, square, work],
    )(lengths, frames, proj, grad_out, proj_out, conv_a, buf_a, gain_row, shift_row, counts_row)
    late = lax.optimization_barrier((frames, grad_out, params))
    left_in_a = core_rows(late[0], core)
    left_out_a = core_rows(late[1], core)
    got, left_in_a, left_out_a = lax.optimization_barrier((got, left_in_a, left_out_a))

    hidden_a, stats, sums = call(
        norm_kernel,
        (
            shape((rows, channels), BF16),
            shape((2, channels)),
            shape((3 * (count + 1) + 8, channels)),
        ),
        [SM] + [VM] * 7,
        [work],
    )(lengths, got, params, conv_a, hid_a, buf_a, ones_a, conv_sum_a)
    (pay,) = call(
        spread_kernel, (hbm_shape((chips, 8, LANES)),), [VM, VM], [pltpu.VMEM((3 * (count + 1) + 8, channels), F32)]
    )(sums, swap_cores(sums))
    got = lax.all_to_all(pay, YZ, 0, 0)

    given = after(given, pay)
    value_b, sig_b, hid_b, conv_b, hidden_b, ends = call(
        mirror_kernel,
        (
            hbm_shape((rows, channels)),
            hbm_shape((rows, channels)),
            hbm_shape((rows, channels)),
            full,
            shape((rows, channels), BF16),
            shape((8, LANES)),
        ),
        [HB, HB, HB, HB, VM, VM],
        [wide, square, work],
    )(given, proj, proj_out, taps, stats, params)
    left_in_b = core_rows(given[:rows], core)
    left_out_b = core_rows(given[rows : 2 * rows], core)
    (out_rows,) = call(rows_kernel, (hbm_shape((width // 2, channels), BF16),), [HB, HB, VM, VM])(
        left_out_a, left_out_b, hidden_a, hidden_b
    )
    got, out_rows, left_in_a, left_in_b = lax.optimization_barrier((got, out_rows, left_in_a, left_in_b))
    out_rows = out_rows.reshape(chips, rows_dev, channels)

    half = (chip % 2).astype(jnp.int32).reshape(1)
    grad_pre, shift_grad, gain_grad, pay = call(
        back_kernel,
        (
            shape((rows, 2 * channels), BF16),
            hbm_shape((1, channels)),
            hbm_shape((1, channels)),
            hbm_shape((chips, rows_dev, 3 * channels + LANES), BF16),
        ),
        [SM, SM] + [VM] * 7 + [AN] * 9,
        [
            work,
            pltpu.VMEM((2 * rows, 2 * channels), BF16),
            pltpu.VMEM((2, rows, channels), F32),
            pltpu.VMEM((2, rows, channels), F32),
            pltpu.VMEM((2, rows, channels), F32),
            pltpu.VMEM((2, width // 2, rows), BF16),
            pltpu.VMEM((chips, rows_dev, channels), BF16),
            pltpu.SemaphoreType.DMA((9,)),
        ],
    )(
        lengths, half, ends, got, params, stats, conv_a, conv_b, taps,
        hid_a, hid_b, value_a, value_b, sig_a, sig_b, left_in_a, left_in_b, out_rows,
    )
    got = lax.all_to_all(pay, YZ, 0, 0)

    term = shape((rows, width // groups), BF16)
    own, one, two, three = call(frame_kernel, (term,) * 4, [SM, VM, HB])(
        mp.astype(jnp.int32).reshape(1), grad_pre, proj
    )

    frame_sum = own.astype(F32)
    for d, part in ((1, one), (2, two), (3, three)):
        part = lax.ppermute(after(part, pay), "mp", [(i, (i + d) % groups) for i in range(groups)])
        frame_sum = frame_sum + part.astype(F32)
    frame_grad = frame_sum.astype(BF16)

    in_grad, out_grad, depth_grad = call(
        last_kernel,
        (hbm_shape((rows_dev, 2, channels)), hbm_shape((rows_dev, channels)), hbm_shape((count, channels))),
        [VM],
    )(got)
    return (frame_grad, in_grad, out_grad, depth_grad, gain_grad.reshape(channels), shift_grad.reshape(channels))


def solution(mesh):
    grid = Mesh(mesh.devices.reshape(8, 8, 2, 4), ("y", "z", "core", "mp"))
    placed = (
        P(DP, None),
        P(None, None, "mp"),
        P(None, "mp"),
        P("mp"),
        P("mp"),
        P(None, "mp"),
        P(DP, None),
        P(),
        P(DP, None),
    )
    return jax.shard_map(
        shards,
        mesh=grid,
        in_specs=placed,
        out_specs=(
            P(DP, "mp"),
            P(DP, None, "mp"),
            P(DP, "mp"),
            P(None, "mp"),
            P("mp"),
            P("mp"),
        ),
        check_vma=False,
    )
```

```python
import jax
import jax.numpy as jnp
from jax import lax
from jax.experimental import pallas as pl
from jax.experimental.pallas import tpu as pltpu
from jax.sharding import Mesh, PartitionSpec as P


BLOCK = 128
DP = ("y", "z", "core")
YZ = ("y", "z")
LANES = 128
TAPS = 31
PAD = 16
F32 = jnp.float32
BF16 = jnp.bfloat16
VM = pl.BlockSpec(memory_space=pltpu.VMEM)
HB = pl.BlockSpec(memory_space=pltpu.VMEM)
AN = pl.BlockSpec(memory_space=pl.ANY)
SM = pl.BlockSpec(memory_space=pltpu.SMEM)
NT = (((1,), (1,)), ((), ()))


def call(body, outs, ins, scratch=(), out_specs=None):
    kernel = pl.pallas_call(
        body,
        out_shape=outs,
        in_specs=ins,
        out_specs=out_specs or tuple(VM for _ in outs),
        scratch_shapes=list(scratch),
    )

    def run(*args):
        held = [
            pltpu.with_memory_space_constraint(a, pltpu.VMEM) if spec is VM else a
            for a, spec in zip(args, ins)
        ]
        return kernel(*held)

    return run


def shape(dims, dtype=F32):
    return pltpu.VMEM(dims, dtype)


def hbm_shape(dims, dtype=F32):
    return jax.ShapeDtypeStruct(dims, dtype)


def tree_sum(x):
    while x.shape[0] > 1:
        half = x.shape[0] // 2
        x = x[:half] + x[half:]
    return x[0]


def lanes(h):
    return slice(h * LANES, (h + 1) * LANES)


def row_masks(split, end, rows):
    row = lax.broadcasted_iota(jnp.int32, (rows, LANES), 0).astype(F32)
    return row < split, row < end


def own_masks(len_ref, rows):
    split = len_ref[0, 0]
    return row_masks(split.astype(F32), (split + len_ref[0, 1]).astype(F32), rows)


def embed(buf, h, x, first):
    rows = x.shape[0]
    zero = jnp.zeros((PAD, LANES), F32)
    head = jnp.where(first, x, 0.0)
    tail = jnp.where(first, 0.0, x)
    buf[h, 0:PAD] = zero
    buf[h, PAD : 2 * PAD] = head[:PAD]
    buf[h, 2 * PAD : PAD + rows] = head[PAD:] + tail[: rows - PAD]
    buf[h, PAD + rows : 2 * PAD + rows] = tail[rows - PAD :]
    buf[h, 2 * PAD + rows : 3 * PAD + rows] = zero


def conv(buf, h, taps, rows, first, sign):
    count = taps.shape[0]
    radius = count // 2
    span = rows + PAD
    total = jnp.zeros((span, LANES), F32)
    for k in range(count):
        total = total + taps[k : k + 1, lanes(h)] * buf[h, pl.ds(PAD + sign * (k - radius), span), :]
    return jnp.where(first, total[:rows], total[PAD:])


def tap_sums(out, values, buf, h, count, rows):
    radius = count // 2
    span = rows + PAD
    for k in range(count):
        prod = values * buf[h, pl.ds(PAD + k - radius, span), :]
        out[k : k + 1, lanes(h)] = jnp.sum(prod, axis=0, keepdims=True)


def fetches(sources, targets, sems):
    copies = [pltpu.make_async_copy(a, b, sems.at[i]) for i, (a, b) in enumerate(zip(sources, targets))]
    for copy in copies:
        copy.start()
    return copies


def batch_norm(conv_out, mean, inv_std, params, cols):
    norm = (conv_out[:, cols] - mean[:, cols]) * inv_std[:, cols]
    scaled = norm * params[0:1, cols] + params[1:2, cols]
    return norm, scaled, jax.nn.sigmoid(scaled)


def swish_slope(scaled, s):
    return s * (1.0 + scaled * (1.0 - s))


def gated(pre, live, h, channels):
    value = pre[:, lanes(h)]
    sig = jax.nn.sigmoid(pre[:, channels + h * LANES : channels + (h + 1) * LANES])
    return value, sig, jnp.where(live, value * sig, 0.0).astype(BF16).astype(F32)


def forward_kernel(
    len_ref, frames, proj, taps, raw_frames, raw_grad,
    conv_out, buf, pay, value_out, sig_out, given, pre, value, sig, spans, sems,
):
    rows, channels = conv_out.shape
    first, live = own_masks(len_ref, rows)
    lane = lax.broadcasted_iota(jnp.int32, spans.shape, 1)
    spans[...] = jnp.where(
        lane == 0, len_ref[0, 0].astype(F32), jnp.where(lane == 1, len_ref[0, 1].astype(F32), 0.0)
    ).astype(BF16)
    copies = fetches(
        (raw_frames, raw_grad, spans),
        (given.at[pl.ds(0, rows)], given.at[pl.ds(rows, rows)], given.at[pl.ds(2 * rows, 16)]),
        sems,
    )
    pre[...] = jnp.dot(frames[...], proj[...], preferred_element_type=F32)
    glus = []
    for h in range(channels // LANES):
        value[:, lanes(h)], sig[:, lanes(h)], glu = gated(pre, live, h, channels)
        glus.append(glu)
    copies += fetches((value, sig), (value_out, sig_out), sems.at[pl.ds(3, 2)])
    sums = []
    for h, glu in enumerate(glus):
        embed(buf, h, glu, first)
        out = jnp.where(live, conv(buf, h, taps, rows, first, 1), 0.0)
        conv_out[:, lanes(h)] = out
        sums.append(
            jnp.concatenate(
                [jnp.sum(out, axis=0, keepdims=True), jnp.sum(out * out, axis=0, keepdims=True)], axis=0
            )
        )
    both = jnp.concatenate(sums, axis=1)
    pay[...] = jnp.broadcast_to(both[None], pay.shape)
    for copy in copies:
        copy.wait()


def live_taps(split, end, rows):
    dims = (TAPS + 1, rows + 3 * PAD)
    tap = lax.broadcasted_iota(jnp.int32, dims, 0)
    at = lax.broadcasted_iota(jnp.int32, dims, 1) - tap + TAPS // 2
    one = (at >= PAD) & (at < PAD + split)
    two = (at >= 2 * PAD + split) & (at < 2 * PAD + end)
    return jnp.where(one | two, 1.0, 0.0).astype(BF16)


def side_kernel(
    len_ref, grad_out, proj_out, conv_out, buf, gain, shift, counts,
    grad_hidden, ones_sum, conv_sum, params, hid, work,
):
    rows, channels = conv_out.shape
    first, live = own_masks(len_ref, rows)
    marks = live_taps(len_ref[0, 0], len_ref[0, 0] + len_ref[0, 1], rows)
    hid[...] = jnp.dot(grad_out[...], proj_out[...], preferred_element_type=F32)
    for h in range(channels // LANES):
        cols = lanes(h)
        grad_hidden[:, cols] = jnp.where(live, hid[:, cols], 0.0)
        ones_sum[:, cols] = jnp.dot(marks, buf[h].astype(BF16), preferred_element_type=F32)
        embed(work, h, conv_out[:, cols], first)
        tap_sums(conv_sum, work[h, pl.ds(PAD, rows + PAD), :], buf, h, TAPS, rows)
        conv_sum[TAPS : TAPS + 1, cols] = jnp.zeros((1, LANES), F32)
    total = jnp.sum(counts[...].astype(F32), axis=1, keepdims=True) * BLOCK
    params[0:1] = gain[...]
    params[1:2] = shift[...]
    params[2:3] = jnp.broadcast_to(total, (1, channels))
    params[3:] = jnp.zeros((5, channels), F32)


def mirror_kernel(
    given, proj, proj_out, taps, stats, params,
    value, sig, grad_hidden, conv_out, hidden, ends, pre, hid, buf,
):
    rows, channels = conv_out.shape
    spans = given[2 * rows : 2 * rows + 16, :LANES].astype(F32)[0:1]
    split = spans[:, 0:1]
    end = split + spans[:, 1:2]
    ends[0:1] = jnp.broadcast_to(split, (1, LANES))
    ends[1:2] = jnp.broadcast_to(end, (1, LANES))
    ends[2:] = jnp.zeros((6, LANES), F32)
    first, live = row_masks(ends[0:1], ends[1:2], rows)
    mean, inv_std = stats[0:1], stats[1:2]
    pre[...] = jnp.dot(given[:rows], proj[...], preferred_element_type=F32)
    hid[...] = jnp.dot(given[rows : 2 * rows], proj_out[...], preferred_element_type=F32)
    for h in range(channels // LANES):
        cols = lanes(h)
        value[:, cols], sig[:, cols], glu = gated(pre, live, h, channels)
        embed(buf, h, glu, first)
        conv_out[:, cols] = jnp.where(live, conv(buf, h, taps, rows, first, 1), 0.0)
        grad_hidden[:, cols] = jnp.where(live, hid[:, cols], 0.0)
        _, scaled, s = batch_norm(conv_out, mean, inv_std, params, cols)
        hidden[:, cols] = jnp.where(live, scaled * s, 0.0).astype(BF16)


def norm_kernel(
    len_ref, got, params, conv_out, grad_hidden, buf, ones_sum, conv_sum,
    hidden, stats, sums, work,
):
    rows, channels = conv_out.shape
    count = TAPS
    first, live = own_masks(len_ref, rows)
    total = params[2:3]
    found = tree_sum(got[...])
    mean = found[0:1] / total
    inv_std = lax.rsqrt(found[1:2] / total - mean * mean + 1e-05)
    stats[0:1] = mean
    stats[1:2] = inv_std
    base = 3 * (count + 1)
    sums[count + 1 : 2 * (count + 1)] = ones_sum[...]
    sums[2 * (count + 1) : base] = conv_sum[...]
    sums[base + 2 :] = jnp.zeros((6, channels), F32)
    for h in range(channels // LANES):
        cols = lanes(h)
        norm, scaled, s = batch_norm(conv_out, mean, inv_std, params, cols)
        hidden[:, cols] = jnp.where(live, scaled * s, 0.0).astype(BF16)
        grad = grad_hidden[:, cols] * swish_slope(scaled, s)
        sums[base : base + 1, cols] = jnp.sum(grad, axis=0, keepdims=True)
        sums[base + 1 : base + 2, cols] = jnp.sum(grad * norm, axis=0, keepdims=True)
        embed(work, h, grad, first)
        tap_sums(sums, work[h, pl.ds(PAD, rows + PAD), :], buf, h, count, rows)
        sums[count : count + 1, cols] = jnp.zeros((1, LANES), F32)


def spread_kernel(own, other, pay, sums):
    sums[...] = own[...] + other[...]
    count = pay.shape[0] // 2
    base = 3 * count
    tile = jnp.concatenate(
        [sums[base + i : base + i + 1, lanes(h)] for i in range(2) for h in range(2)]
        + [jnp.zeros((4, LANES), F32)],
        axis=0,
    )
    pay[...] = jnp.broadcast_to(tile[None], pay.shape)
    for j in range(pay.shape[0]):
        for i in range(3):
            at = i * count + j // 2
            pay[j, 4 + i : 5 + i, :] = sums[at : at + 1, lanes(j % 2)]


def back_kernel(
    len_ref, half_ref, ends, got, params, stats, conv_a, conv_b, taps,
    hid_a, hid_b, value_a, value_b, sig_a, sig_b, left_a, left_b, rows_in,
    own_pre, shift_grad, gain_grad, pay, work, grad_pre, hids, values, sigs, left, out_rows, sems,
):
    rows, channels = conv_a.shape
    width = 2 * channels
    peers, rows_dev, _ = pay.shape
    copies = fetches(
        (hid_a, hid_b, value_a, value_b, sig_a, sig_b, left_a, left_b, rows_in),
        (
            hids.at[0], hids.at[1], values.at[0], values.at[1], sigs.at[0], sigs.at[1],
            left.at[0], left.at[1], out_rows,
        ),
        sems,
    )
    total = params[2:3]
    sums = tree_sum(got[...])
    mean, inv_std = stats[0:1], stats[1:2]
    slices, scales, means = [], [], []
    for h in range(channels // LANES):
        cols = lanes(h)
        s, q = sums[h : h + 1], sums[2 + h : 3 + h]
        shift_grad[:, cols] = s
        gain_grad[:, cols] = q
        scale = params[0:1, cols] * inv_std[:, cols]
        s, q = s / total[:, cols], q / total[:, cols]
        own, ones, cv = sums[4:5], sums[5:6], sums[6:7]
        slices.append(scale * (own - s * ones - q * inv_std[:, cols] * (cv - mean[:, cols] * ones)))
        scales.append(scale)
        means.append((s, q))
    for part, conv_out in enumerate((conv_a, conv_b)):
        masks = own_masks(len_ref, rows) if part == 0 else row_masks(ends[0:1], ends[1:2], rows)
        first, live = masks
        span = slice(part * rows, (part + 1) * rows)
        copies[part].wait()
        for h in range(channels // LANES):
            cols = lanes(h)
            s, q = means[h]
            norm, scaled, swish = batch_norm(conv_out, mean, inv_std, params, cols)
            grad = scales[h] * (hids[part, :, cols] * swish_slope(scaled, swish) - s - norm * q)
            embed(work, h, jnp.where(live, grad, 0.0), first)
            glu = jnp.where(live, conv(work, h, taps, rows, first, -1), 0.0)
            if h == 0:
                copies[2 + part].wait()
                copies[4 + part].wait()
            v, g = values[part, :, cols], sigs[part, :, cols]
            grad_pre[span, cols] = (glu * g).astype(BF16)
            grad_pre[span, channels + h * LANES : channels + (h + 1) * LANES] = (
                glu * v * g * (1.0 - g)
            ).astype(BF16)
        copies[6 + part].wait()
        term = jnp.dot(left[part], grad_pre[span], preferred_element_type=F32)
        total = term if part == 0 else total + term
    own_pre[...] = grad_pre[:rows]
    which = jnp.full((1, LANES), half_ref[0], jnp.int32)
    depth = jnp.where(which == 0, slices[0], slices[1]).astype(BF16)
    copies[8].wait()
    pay[:, :, :width] = total.reshape(peers, rows_dev, width).astype(BF16)
    pay[:, :, width : width + channels] = out_rows[...]
    pay[:, :, width + channels :] = jnp.broadcast_to(depth[None], (peers, rows_dev, LANES))


def frame_kernel(mp_ref, grad_pre, proj, own, one, two, three):
    width = own.shape[1]
    groups = proj.shape[0] // width
    for d, out in enumerate((own, one, two, three)):
        at = pl.multiple_of(lax.rem(mp_ref[0] + d, groups) * width, width)
        term = lax.dot_general(grad_pre[...], proj[pl.ds(at, width), :], NT, preferred_element_type=F32)
        out[...] = term.astype(BF16)


def rows_kernel(left_a, left_b, right_a, right_b, out):
    total = jnp.dot(left_a[...], right_a[...], preferred_element_type=F32)
    total = total + jnp.dot(left_b[...], right_b[...], preferred_element_type=F32)
    out[...] = total.astype(BF16)


def last_kernel(got, in_rows, out_rows, depth):
    more = out_rows.shape[1]
    width = 2 * more
    for g in range(2):
        total = jnp.zeros((in_rows.shape[0], more), F32)
        for j in range(got.shape[0]):
            total = total + got[j, :, g * more : (g + 1) * more].astype(F32)
        in_rows[:, g, :] = total
    total = jnp.zeros((in_rows.shape[0], more), F32)
    for j in range(got.shape[0]):
        total = total + got[j, :, width : width + more].astype(F32)
    out_rows[...] = total
    for j in range(2 * depth.shape[0]):
        depth[j // 2 : j // 2 + 1, lanes(j % 2)] = got[j, 0:1, width + more :].astype(F32)


def core_rows(x, core):
    frames, width = x.shape
    rows = x.T.reshape(width // 16, 2, 8, frames)
    return lax.dynamic_index_in_dim(rows, core, 1, keepdims=False).reshape(width // 2, frames)


def swap_cores(x):
    return lax.ppermute(x, "core", [(0, 1), (1, 0)])


def after(x, y):
    return lax.optimization_barrier((x, y))[0]


def shards(frames, proj_in, taps, bn_gain, bn_shift, proj_out, grad_out, counts, lengths):
    rows, width = frames.shape
    channels = proj_in.shape[2]
    count = taps.shape[0]
    halves = channels // LANES
    buf_rows = rows + 3 * PAD
    peers = lax.axis_size(DP)
    chips = lax.axis_size(YZ)
    groups = lax.axis_size("mp")
    rows_dev = width // peers
    core = lax.axis_index("core")
    chip = lax.axis_index(YZ)
    mp = lax.axis_index("mp")
    full = shape((rows, channels))
    buf_shape = (halves, buf_rows, LANES)
    tap_shape = (count + 1, channels)
    wide = pltpu.VMEM((rows, 2 * channels), F32)
    square = pltpu.VMEM((rows, channels), F32)
    work = pltpu.VMEM(buf_shape, F32)
    proj = proj_in.reshape(width, 2 * channels)
    counts_row = counts.reshape(1, -1)
    gain_row = bn_gain.reshape(1, channels)
    shift_row = bn_shift.reshape(1, channels)

    conv_a, buf_a, pay, value_a, sig_a, given = call(
        forward_kernel,
        (
            full,
            shape(buf_shape),
            hbm_shape((peers, 2, channels)),
            hbm_shape((rows, channels)),
            hbm_shape((rows, channels)),
            hbm_shape((2 * rows + 16, width), BF16),
        ),
        [SM, VM, VM, VM, AN, AN],
        [wide, square, square, pltpu.VMEM((16, width), BF16), pltpu.SemaphoreType.DMA((5,))],
        out_specs=(VM, VM, VM, AN, AN, AN),
    )(lengths, frames, proj, taps, frames, grad_out)
    got = lax.all_to_all(pay, DP, 0, 0)

    given = swap_cores(given)
    hid_a, ones_a, conv_sum_a, params = call(
        side_kernel,
        (
            full,
            shape(tap_shape),
            shape(tap_shape),
            shape((8, channels)),
        ),
        [SM, HB, HB, VM, VM, HB, HB, HB],
        [square, work],
    )(lengths, grad_out, proj_out, conv_a, buf_a, gain_row, shift_row, counts_row)
    late = lax.optimization_barrier((frames, grad_out, params))
    left_in_a = core_rows(late[0], core)
    left_out_a = core_rows(late[1], core)
    got, left_in_a, left_out_a = lax.optimization_barrier((got, left_in_a, left_out_a))

    hidden_a, stats, sums = call(
        norm_kernel,
        (
            shape((rows, channels), BF16),
            shape((2, channels)),
            shape((3 * (count + 1) + 8, channels)),
        ),
        [SM] + [VM] * 7,
        [work],
    )(lengths, got, params, conv_a, hid_a, buf_a, ones_a, conv_sum_a)
    (pay,) = call(
        spread_kernel,
        (hbm_shape((chips, 8, LANES)),),
        [VM, VM],
        [pltpu.VMEM((3 * (count + 1) + 8, channels), F32)],
    )(sums, swap_cores(sums))
    got = lax.all_to_all(pay, YZ, 0, 0)

    given = after(given, pay)
    value_b, sig_b, hid_b, conv_b, hidden_b, ends = call(
        mirror_kernel,
        (
            hbm_shape((rows, channels)),
            hbm_shape((rows, channels)),
            hbm_shape((rows, channels)),
            full,
            shape((rows, channels), BF16),
            shape((8, LANES)),
        ),
        [HB, HB, HB, HB, VM, VM],
        [wide, square, work],
    )(given, proj, proj_out, taps, stats, params)
    left_in_b = core_rows(given[:rows], core)
    left_out_b = core_rows(given[rows : 2 * rows], core)
    (out_rows,) = call(rows_kernel, (hbm_shape((width // 2, channels), BF16),), [HB, HB, VM, VM])(
        left_out_a, left_out_b, hidden_a, hidden_b
    )
    got, out_rows, left_in_a, left_in_b = lax.optimization_barrier((got, out_rows, left_in_a, left_in_b))
    out_rows = out_rows.reshape(chips, rows_dev, channels)

    half = (chip % 2).astype(jnp.int32).reshape(1)
    grad_pre, shift_grad, gain_grad, pay = call(
        back_kernel,
        (
            shape((rows, 2 * channels), BF16),
            hbm_shape((1, channels)),
            hbm_shape((1, channels)),
            hbm_shape((chips, rows_dev, 3 * channels + LANES), BF16),
        ),
        [SM, SM] + [VM] * 7 + [AN] * 9,
        [
            work,
            pltpu.VMEM((2 * rows, 2 * channels), BF16),
            pltpu.VMEM((2, rows, channels), F32),
            pltpu.VMEM((2, rows, channels), F32),
            pltpu.VMEM((2, rows, channels), F32),
            pltpu.VMEM((2, width // 2, rows), BF16),
            pltpu.VMEM((chips, rows_dev, channels), BF16),
            pltpu.SemaphoreType.DMA((9,)),
        ],
    )(
        lengths, half, ends, got, params, stats, conv_a, conv_b, taps,
        hid_a, hid_b, value_a, value_b, sig_a, sig_b, left_in_a, left_in_b, out_rows,
    )
    got = lax.all_to_all(pay, YZ, 0, 0)

    term = shape((rows, width // groups), BF16)
    own, one, two, three = call(frame_kernel, (term,) * 4, [SM, VM, HB])(
        mp.astype(jnp.int32).reshape(1), grad_pre, proj
    )

    frame_sum = own.astype(F32)
    for d, part in ((1, one), (2, two), (3, three)):
        part = lax.ppermute(after(part, pay), "mp", [(i, (i + d) % groups) for i in range(groups)])
        frame_sum = frame_sum + part.astype(F32)
    frame_grad = frame_sum.astype(BF16)

    in_grad, out_grad, depth_grad = call(
        last_kernel,
        (hbm_shape((rows_dev, 2, channels)), hbm_shape((rows_dev, channels)), hbm_shape((count, channels))),
        [VM],
    )(got)
    return (frame_grad, in_grad, out_grad, depth_grad, gain_grad.reshape(channels), shift_grad.reshape(channels))


def solution(mesh):
    grid = Mesh(mesh.devices.reshape(8, 8, 2, 4), ("y", "z", "core", "mp"))
    placed = (
        P(DP, None),
        P(None, None, "mp"),
        P(None, "mp"),
        P("mp"),
        P("mp"),
        P(None, "mp"),
        P(DP, None),
        P(),
        P(DP, None),
    )
    return jax.shard_map(
        shards,
        mesh=grid,
        in_specs=placed,
        out_specs=(
            P(DP, "mp"),
            P(DP, None, "mp"),
            P(DP, "mp"),
            P(None, "mp"),
            P("mp"),
            P("mp"),
        ),
        check_vma=False,
    )
```

```python
import jax
import jax.numpy as jnp
from jax import lax
from jax.experimental import pallas as pl
from jax.experimental.pallas import tpu as pltpu
from jax.sharding import Mesh, PartitionSpec as P


BLOCK = 128
DP = ("y", "z", "core")
YZ = ("y", "z")
LANES = 128
TAPS = 31
PAD = 16
F32 = jnp.float32
BF16 = jnp.bfloat16
VM = pl.BlockSpec(memory_space=pltpu.VMEM)
HB = pl.BlockSpec(memory_space=pltpu.VMEM)
AN = pl.BlockSpec(memory_space=pl.ANY)
SM = pl.BlockSpec(memory_space=pltpu.SMEM)
NT = (((1,), (1,)), ((), ()))


def call(body, outs, ins, scratch=(), out_specs=None):
    kernel = pl.pallas_call(
        body, out_shape=outs, in_specs=ins, out_specs=out_specs or tuple(VM for _ in outs), scratch_shapes=list(scratch)
    )

    def run(*args):
        held = [
            pltpu.with_memory_space_constraint(a, pltpu.VMEM) if spec is VM else a
            for a, spec in zip(args, ins)
        ]
        return kernel(*held)

    return run


def shape(dims, dtype=F32):
    return pltpu.VMEM(dims, dtype)


def hbm_shape(dims, dtype=F32):
    return jax.ShapeDtypeStruct(dims, dtype)


def tree_sum(x):
    while x.shape[0] > 1:
        half = x.shape[0] // 2
        x = x[:half] + x[half:]
    return x[0]


def lanes(h):
    return slice(h * LANES, (h + 1) * LANES)


def row_masks(split, end, rows):
    row = lax.broadcasted_iota(jnp.int32, (rows, LANES), 0).astype(F32)
    return row < split, row < end


def own_masks(len_ref, rows):
    split = len_ref[0, 0]
    return row_masks(split.astype(F32), (split + len_ref[0, 1]).astype(F32), rows)


def embed(buf, h, x, first):
    rows = x.shape[0]
    zero = jnp.zeros((PAD, LANES), F32)
    head = jnp.where(first, x, 0.0)
    tail = jnp.where(first, 0.0, x)
    buf[h, 0:PAD] = zero
    buf[h, PAD : 2 * PAD] = head[:PAD]
    buf[h, 2 * PAD : PAD + rows] = head[PAD:] + tail[: rows - PAD]
    buf[h, PAD + rows : 2 * PAD + rows] = tail[rows - PAD :]
    buf[h, 2 * PAD + rows : 3 * PAD + rows] = zero


def conv(buf, h, taps, rows, first, sign):
    count = taps.shape[0]
    radius = count // 2
    span = rows + PAD
    total = jnp.zeros((span, LANES), F32)
    for k in range(count):
        total = total + taps[k : k + 1, lanes(h)] * buf[h, pl.ds(PAD + sign * (k - radius), span), :]
    return jnp.where(first, total[:rows], total[PAD:])


def tap_sums(out, values, buf, h, count, rows):
    radius = count // 2
    span = rows + PAD
    for k in range(count):
        prod = values * buf[h, pl.ds(PAD + k - radius, span), :]
        out[k : k + 1, lanes(h)] = jnp.sum(prod, axis=0, keepdims=True)


def fetches(sources, targets, sems):
    copies = [pltpu.make_async_copy(a, b, sems.at[i]) for i, (a, b) in enumerate(zip(sources, targets))]
    for copy in copies:
        copy.start()
    return copies


def batch_norm(conv_out, mean, inv_std, params, cols):
    norm = (conv_out[:, cols] - mean[:, cols]) * inv_std[:, cols]
    scaled = norm * params[0:1, cols] + params[1:2, cols]
    return norm, scaled, jax.nn.sigmoid(scaled)


def swish_slope(scaled, s):
    return s * (1.0 + scaled * (1.0 - s))


def gated(pre, live, h, channels):
    value = pre[:, lanes(h)]
    sig = jax.nn.sigmoid(pre[:, channels + h * LANES : channels + (h + 1) * LANES])
    return value, sig, jnp.where(live, value * sig, 0.0).astype(BF16).astype(F32)


def forward_kernel(
    len_ref, frames, proj, taps, raw_grad,
    conv_out, buf, pay, value_out, sig_out, given, pre, value, sig, spans, grad, sems,
):
    rows, channels = conv_out.shape
    first, live = own_masks(len_ref, rows)
    lane = lax.broadcasted_iota(jnp.int32, spans.shape, 1)
    spans[...] = jnp.where(
        lane == 0, len_ref[0, 0].astype(F32), jnp.where(lane == 1, len_ref[0, 1].astype(F32), 0.0)
    ).astype(BF16)
    (inward,) = fetches((raw_grad,), (grad,), sems)
    copies = fetches(
        (frames, spans), (given.at[pl.ds(0, rows)], given.at[pl.ds(2 * rows, 16)]), sems.at[pl.ds(1, 2)]
    )
    pre[...] = jnp.dot(frames[...], proj[...], preferred_element_type=F32)
    for h in range(channels // LANES):
        value[:, lanes(h)], sig[:, lanes(h)], glu = gated(pre, live, h, channels)
        embed(buf, h, glu, first)
    copies += fetches((value, sig), (value_out, sig_out), sems.at[pl.ds(3, 2)])
    sums = []
    for h in range(channels // LANES):
        out = jnp.where(live, conv(buf, h, taps, rows, first, 1), 0.0)
        conv_out[:, lanes(h)] = out
        sums.append(
            jnp.concatenate(
                [jnp.sum(out, axis=0, keepdims=True), jnp.sum(out * out, axis=0, keepdims=True)], axis=0
            )
        )
        if h == 0:
            inward.wait()
            copies += fetches((grad,), (given.at[pl.ds(rows, rows)],), sems.at[pl.ds(5, 1)])
    both = jnp.concatenate(sums, axis=1)
    pay[...] = jnp.broadcast_to(both[None], pay.shape)
    for copy in copies:
        copy.wait()


def live_taps(split, end, rows):
    dims = (TAPS + 1, rows + 3 * PAD)
    tap = lax.broadcasted_iota(jnp.int32, dims, 0)
    at = lax.broadcasted_iota(jnp.int32, dims, 1) - tap + TAPS // 2
    one = (at >= PAD) & (at < PAD + split)
    two = (at >= 2 * PAD + split) & (at < 2 * PAD + end)
    return jnp.where(one | two, 1.0, 0.0).astype(BF16)


def side_kernel(
    len_ref, grad_out, proj_out, conv_out, buf, gain, shift, counts,
    grad_hidden, ones_sum, conv_sum, params, hid, work,
):
    rows, channels = conv_out.shape
    first, live = own_masks(len_ref, rows)
    marks = live_taps(len_ref[0, 0], len_ref[0, 0] + len_ref[0, 1], rows)
    hid[...] = jnp.dot(grad_out[...], proj_out[...], preferred_element_type=F32)
    for h in range(channels // LANES):
        cols = lanes(h)
        grad_hidden[:, cols] = jnp.where(live, hid[:, cols], 0.0)
        ones_sum[:, cols] = jnp.dot(marks, buf[h].astype(BF16), preferred_element_type=F32)
        embed(work, h, conv_out[:, cols], first)
        tap_sums(conv_sum, work[h, pl.ds(PAD, rows + PAD), :], buf, h, TAPS, rows)
        conv_sum[TAPS : TAPS + 1, cols] = jnp.zeros((1, LANES), F32)
    total = jnp.sum(counts[...].astype(F32), axis=1, keepdims=True) * BLOCK
    params[0:1] = gain[...]
    params[1:2] = shift[...]
    params[2:3] = jnp.broadcast_to(total, (1, channels))
    params[3:] = jnp.zeros((5, channels), F32)


def mirror_kernel(
    given, proj, proj_out, taps, stats, params,
    value, sig, grad_hidden, conv_out, hidden, ends, pre, hid, buf,
):
    rows, channels = conv_out.shape
    spans = given[2 * rows : 2 * rows + 16, :LANES].astype(F32)[0:1]
    split = spans[:, 0:1]
    end = split + spans[:, 1:2]
    ends[0:1] = jnp.broadcast_to(split, (1, LANES))
    ends[1:2] = jnp.broadcast_to(end, (1, LANES))
    ends[2:] = jnp.zeros((6, LANES), F32)
    first, live = row_masks(ends[0:1], ends[1:2], rows)
    mean, inv_std = stats[0:1], stats[1:2]
    pre[...] = jnp.dot(given[:rows], proj[...], preferred_element_type=F32)
    hid[...] = jnp.dot(given[rows : 2 * rows], proj_out[...], preferred_element_type=F32)
    for h in range(channels // LANES):
        cols = lanes(h)
        value[:, cols], sig[:, cols], glu = gated(pre, live, h, channels)
        embed(buf, h, glu, first)
        conv_out[:, cols] = jnp.where(live, conv(buf, h, taps, rows, first, 1), 0.0)
        grad_hidden[:, cols] = jnp.where(live, hid[:, cols], 0.0)
        _, scaled, s = batch_norm(conv_out, mean, inv_std, params, cols)
        hidden[:, cols] = jnp.where(live, scaled * s, 0.0).astype(BF16)


def norm_kernel(
    len_ref, got, params, conv_out, grad_hidden, buf, ones_sum, conv_sum,
    hidden, stats, sums, work,
):
    rows, channels = conv_out.shape
    count = TAPS
    first, live = own_masks(len_ref, rows)
    total = params[2:3]
    found = tree_sum(got[...])
    mean = found[0:1] / total
    inv_std = lax.rsqrt(found[1:2] / total - mean * mean + 1e-05)
    stats[0:1] = mean
    stats[1:2] = inv_std
    base = 3 * (count + 1)
    sums[count + 1 : 2 * (count + 1)] = ones_sum[...]
    sums[2 * (count + 1) : base] = conv_sum[...]
    sums[base + 2 :] = jnp.zeros((6, channels), F32)
    for h in range(channels // LANES):
        cols = lanes(h)
        norm, scaled, s = batch_norm(conv_out, mean, inv_std, params, cols)
        hidden[:, cols] = jnp.where(live, scaled * s, 0.0).astype(BF16)
        grad = grad_hidden[:, cols] * swish_slope(scaled, s)
        sums[base : base + 1, cols] = jnp.sum(grad, axis=0, keepdims=True)
        sums[base + 1 : base + 2, cols] = jnp.sum(grad * norm, axis=0, keepdims=True)
        embed(work, h, grad, first)
        tap_sums(sums, work[h, pl.ds(PAD, rows + PAD), :], buf, h, count, rows)
        sums[count : count + 1, cols] = jnp.zeros((1, LANES), F32)


def spread_kernel(own, other, pay, sums):
    sums[...] = own[...] + other[...]
    count = pay.shape[0] // 2
    base = 3 * count
    tile = jnp.concatenate(
        [sums[base + i : base + i + 1, lanes(h)] for i in range(2) for h in range(2)]
        + [jnp.zeros((4, LANES), F32)],
        axis=0,
    )
    pay[...] = jnp.broadcast_to(tile[None], pay.shape)
    for j in range(pay.shape[0]):
        for i in range(3):
            at = i * count + j // 2
            pay[j, 4 + i : 5 + i, :] = sums[at : at + 1, lanes(j % 2)]


def back_kernel(
    len_ref, half_ref, ends, got, params, stats, conv_a, conv_b, taps,
    hid_a, hid_b, value_a, value_b, sig_a, sig_b, left_a, left_b, rows_in,
    own_pre, shift_grad, gain_grad, pay, work, grad_pre, hids, values, sigs, left, out_rows, sems,
):
    rows, channels = conv_a.shape
    width = 2 * channels
    peers, rows_dev, _ = pay.shape
    copies = fetches(
        (hid_a, hid_b, value_a, value_b, sig_a, sig_b, left_a, left_b, rows_in),
        (
            hids.at[0], hids.at[1], values.at[0], values.at[1], sigs.at[0], sigs.at[1],
            left.at[0], left.at[1], out_rows,
        ),
        sems,
    )
    total = params[2:3]
    sums = tree_sum(got[...])
    mean, inv_std = stats[0:1], stats[1:2]
    slices, scales, means = [], [], []
    for h in range(channels // LANES):
        cols = lanes(h)
        s, q = sums[h : h + 1], sums[2 + h : 3 + h]
        shift_grad[:, cols] = s
        gain_grad[:, cols] = q
        scale = params[0:1, cols] * inv_std[:, cols]
        s, q = s / total[:, cols], q / total[:, cols]
        own, ones, cv = sums[4:5], sums[5:6], sums[6:7]
        slices.append(scale * (own - s * ones - q * inv_std[:, cols] * (cv - mean[:, cols] * ones)))
        scales.append(scale)
        means.append((s, q))
    for part, conv_out in enumerate((conv_a, conv_b)):
        masks = own_masks(len_ref, rows) if part == 0 else row_masks(ends[0:1], ends[1:2], rows)
        first, live = masks
        span = slice(part * rows, (part + 1) * rows)
        copies[part].wait()
        for h in range(channels // LANES):
            cols = lanes(h)
            s, q = means[h]
            norm, scaled, swish = batch_norm(conv_out, mean, inv_std, params, cols)
            grad = scales[h] * (hids[part, :, cols] * swish_slope(scaled, swish) - s - norm * q)
            embed(work, h, jnp.where(live, grad, 0.0), first)
            glu = jnp.where(live, conv(work, h, taps, rows, first, -1), 0.0)
            if h == 0:
                copies[2 + part].wait()
                copies[4 + part].wait()
            v, g = values[part, :, cols], sigs[part, :, cols]
            grad_pre[span, cols] = (glu * g).astype(BF16)
            grad_pre[span, channels + h * LANES : channels + (h + 1) * LANES] = (
                glu * v * g * (1.0 - g)
            ).astype(BF16)
        copies[6 + part].wait()
        term = jnp.dot(left[part], grad_pre[span], preferred_element_type=F32)
        total = term if part == 0 else total + term
    own_pre[...] = grad_pre[:rows]
    which = jnp.full((1, LANES), half_ref[0], jnp.int32)
    depth = jnp.where(which == 0, slices[0], slices[1]).astype(BF16)
    copies[8].wait()
    pay[:, :, :width] = total.reshape(peers, rows_dev, width).astype(BF16)
    pay[:, :, width : width + channels] = out_rows[...]
    pay[:, :, width + channels :] = jnp.broadcast_to(depth[None], (peers, rows_dev, LANES))


def frame_kernel(mp_ref, grad_pre, proj, own, one, two, three):
    width = own.shape[1]
    groups = proj.shape[0] // width
    for d, out in enumerate((own, one, two, three)):
        at = pl.multiple_of(lax.rem(mp_ref[0] + d, groups) * width, width)
        term = lax.dot_general(grad_pre[...], proj[pl.ds(at, width), :], NT, preferred_element_type=F32)
        out[...] = term.astype(BF16)


def rows_kernel(left_a, left_b, right_a, right_b, out):
    total = jnp.dot(left_a[...], right_a[...], preferred_element_type=F32)
    total = total + jnp.dot(left_b[...], right_b[...], preferred_element_type=F32)
    out[...] = total.astype(BF16)


def last_kernel(got, in_rows, out_rows, depth):
    more = out_rows.shape[1]
    width = 2 * more
    for g in range(2):
        total = jnp.zeros((in_rows.shape[0], more), F32)
        for j in range(got.shape[0]):
            total = total + got[j, :, g * more : (g + 1) * more].astype(F32)
        in_rows[:, g, :] = total
    total = jnp.zeros((in_rows.shape[0], more), F32)
    for j in range(got.shape[0]):
        total = total + got[j, :, width : width + more].astype(F32)
    out_rows[...] = total
    for j in range(2 * depth.shape[0]):
        depth[j // 2 : j // 2 + 1, lanes(j % 2)] = got[j, 0:1, width + more :].astype(F32)


def core_rows(x, core):
    frames, width = x.shape
    rows = x.T.reshape(width // 16, 2, 8, frames)
    return lax.dynamic_index_in_dim(rows, core, 1, keepdims=False).reshape(width // 2, frames)


def swap_cores(x):
    return lax.ppermute(x, "core", [(0, 1), (1, 0)])


def after(x, y):
    return lax.optimization_barrier((x, y))[0]


def shards(frames, proj_in, taps, bn_gain, bn_shift, proj_out, grad_out, counts, lengths):
    rows, width = frames.shape
    channels = proj_in.shape[2]
    count = taps.shape[0]
    halves = channels // LANES
    buf_rows = rows + 3 * PAD
    peers = lax.axis_size(DP)
    chips = lax.axis_size(YZ)
    groups = lax.axis_size("mp")
    rows_dev = width // peers
    core = lax.axis_index("core")
    chip = lax.axis_index(YZ)
    mp = lax.axis_index("mp")
    full = shape((rows, channels))
    buf_shape = (halves, buf_rows, LANES)
    tap_shape = (count + 1, channels)
    wide = pltpu.VMEM((rows, 2 * channels), F32)
    square = pltpu.VMEM((rows, channels), F32)
    work = pltpu.VMEM(buf_shape, F32)
    proj = proj_in.reshape(width, 2 * channels)
    counts_row = counts.reshape(1, -1)
    gain_row = bn_gain.reshape(1, channels)
    shift_row = bn_shift.reshape(1, channels)

    conv_a, buf_a, pay, value_a, sig_a, given = call(
        forward_kernel,
        (
            full,
            shape(buf_shape),
            hbm_shape((peers, 2, channels)),
            hbm_shape((rows, channels)),
            hbm_shape((rows, channels)),
            hbm_shape((2 * rows + 16, width), BF16),
        ),
        [SM, VM, VM, VM, AN],
        [
            wide,
            square,
            square,
            pltpu.VMEM((16, width), BF16),
            pltpu.VMEM((rows, width), BF16),
            pltpu.SemaphoreType.DMA((6,)),
        ],
        out_specs=(VM, VM, VM, AN, AN, AN),
    )(lengths, frames, proj, taps, grad_out)
    got = lax.all_to_all(pay, DP, 0, 0)

    given = swap_cores(given)
    hid_a, ones_a, conv_sum_a, params = call(
        side_kernel,
        (
            full,
            shape(tap_shape),
            shape(tap_shape),
            shape((8, channels)),
        ),
        [SM, HB, HB, VM, VM, HB, HB, HB],
        [square, work],
    )(lengths, grad_out, proj_out, conv_a, buf_a, gain_row, shift_row, counts_row)
    late = lax.optimization_barrier((frames, grad_out, params))
    left_in_a = core_rows(late[0], core)
    left_out_a = core_rows(late[1], core)
    got, left_in_a, left_out_a = lax.optimization_barrier((got, left_in_a, left_out_a))

    hidden_a, stats, sums = call(
        norm_kernel,
        (
            shape((rows, channels), BF16),
            shape((2, channels)),
            shape((3 * (count + 1) + 8, channels)),
        ),
        [SM] + [VM] * 7,
        [work],
    )(lengths, got, params, conv_a, hid_a, buf_a, ones_a, conv_sum_a)
    (pay,) = call(
        spread_kernel, (hbm_shape((chips, 8, LANES)),), [VM, VM], [pltpu.VMEM((3 * (count + 1) + 8, channels), F32)]
    )(sums, swap_cores(sums))
    got = lax.all_to_all(pay, YZ, 0, 0)

    given = after(given, pay)
    value_b, sig_b, hid_b, conv_b, hidden_b, ends = call(
        mirror_kernel,
        (
            hbm_shape((rows, channels)),
            hbm_shape((rows, channels)),
            hbm_shape((rows, channels)),
            full,
            shape((rows, channels), BF16),
            shape((8, LANES)),
        ),
        [HB, HB, HB, HB, VM, VM],
        [wide, square, work],
    )(given, proj, proj_out, taps, stats, params)
    left_in_b = core_rows(given[:rows], core)
    left_out_b = core_rows(given[rows : 2 * rows], core)
    (out_rows,) = call(rows_kernel, (hbm_shape((width // 2, channels), BF16),), [HB, VM, VM, VM])(
        left_out_a, left_out_b, hidden_a, hidden_b
    )
    got, out_rows, left_in_a, left_in_b = lax.optimization_barrier((got, out_rows, left_in_a, left_in_b))
    out_rows = out_rows.reshape(chips, rows_dev, channels)

    half = (chip % 2).astype(jnp.int32).reshape(1)
    grad_pre, shift_grad, gain_grad, pay = call(
        back_kernel,
        (
            shape((rows, 2 * channels), BF16),
            hbm_shape((1, channels)),
            hbm_shape((1, channels)),
            hbm_shape((chips, rows_dev, 3 * channels + LANES), BF16),
        ),
        [SM, SM] + [VM] * 7 + [AN] * 9,
        [
            work,
            pltpu.VMEM((2 * rows, 2 * channels), BF16),
            pltpu.VMEM((2, rows, channels), F32),
            pltpu.VMEM((2, rows, channels), F32),
            pltpu.VMEM((2, rows, channels), F32),
            pltpu.VMEM((2, width // 2, rows), BF16),
            pltpu.VMEM((chips, rows_dev, channels), BF16),
            pltpu.SemaphoreType.DMA((9,)),
        ],
    )(
        lengths, half, ends, got, params, stats, conv_a, conv_b, taps,
        hid_a, hid_b, value_a, value_b, sig_a, sig_b, left_in_a, left_in_b, out_rows,
    )
    got = lax.all_to_all(pay, YZ, 0, 0)

    term = shape((rows, width // groups), BF16)
    own, one, two, three = call(frame_kernel, (term,) * 4, [SM, VM, HB])(
        mp.astype(jnp.int32).reshape(1), grad_pre, proj
    )

    frame_sum = own.astype(F32)
    for d, part in ((1, one), (2, two), (3, three)):
        part = lax.ppermute(after(part, pay), "mp", [(i, (i + d) % groups) for i in range(groups)])
        frame_sum = frame_sum + part.astype(F32)
    frame_grad = frame_sum.astype(BF16)

    in_grad, out_grad, depth_grad = call(
        last_kernel,
        (hbm_shape((rows_dev, 2, channels)), hbm_shape((rows_dev, channels)), hbm_shape((count, channels))),
        [VM],
    )(got)
    return (frame_grad, in_grad, out_grad, depth_grad, gain_grad.reshape(channels), shift_grad.reshape(channels))


def solution(mesh):
    grid = Mesh(mesh.devices.reshape(8, 8, 2, 4), ("y", "z", "core", "mp"))
    placed = (
        P(DP, None),
        P(None, None, "mp"),
        P(None, "mp"),
        P("mp"),
        P("mp"),
        P(None, "mp"),
        P(DP, None),
        P(),
        P(DP, None),
    )
    return jax.shard_map(
        shards,
        mesh=grid,
        in_specs=placed,
        out_specs=(
            P(DP, "mp"),
            P(DP, None, "mp"),
            P(DP, "mp"),
            P(None, "mp"),
            P("mp"),
            P("mp"),
        ),
        check_vma=False,
    )
```

```python
import jax
import jax.numpy as jnp
from jax import lax
from jax.experimental import pallas as pl
from jax.experimental.pallas import tpu as pltpu
from jax.sharding import Mesh, PartitionSpec as P


BLOCK = 128
DP = ("y", "z", "core")
YZ = ("y", "z")
LANES = 128
TAPS = 31
PAD = 16
F32 = jnp.float32
BF16 = jnp.bfloat16
VM = pl.BlockSpec(memory_space=pltpu.VMEM)
HB = pl.BlockSpec(memory_space=pltpu.VMEM)
AN = pl.BlockSpec(memory_space=pl.ANY)
SM = pl.BlockSpec(memory_space=pltpu.SMEM)
NT = (((1,), (1,)), ((), ()))


def call(body, outs, ins, scratch=(), out_specs=None):
    kernel = pl.pallas_call(
        body,
        out_shape=outs,
        in_specs=ins,
        out_specs=out_specs or tuple(VM for _ in outs),
        scratch_shapes=list(scratch),
    )

    def run(*args):
        held = [
            pltpu.with_memory_space_constraint(a, pltpu.VMEM) if spec is VM else a
            for a, spec in zip(args, ins)
        ]
        return kernel(*held)

    return run


def shape(dims, dtype=F32):
    return pltpu.VMEM(dims, dtype)


def hbm_shape(dims, dtype=F32):
    return jax.ShapeDtypeStruct(dims, dtype)


def tree_sum(x):
    while x.shape[0] > 1:
        half = x.shape[0] // 2
        x = x[:half] + x[half:]
    return x[0]


def lanes(h):
    return slice(h * LANES, (h + 1) * LANES)


def row_masks(split, end, rows):
    row = lax.broadcasted_iota(jnp.int32, (rows, LANES), 0).astype(F32)
    return row < split, row < end


def own_masks(len_ref, rows):
    split = len_ref[0, 0]
    return row_masks(split.astype(F32), (split + len_ref[0, 1]).astype(F32), rows)


def embed(buf, h, x, first):
    rows = x.shape[0]
    zero = jnp.zeros((PAD, LANES), F32)
    head = jnp.where(first, x, 0.0)
    tail = jnp.where(first, 0.0, x)
    buf[h, 0:PAD] = zero
    buf[h, PAD : 2 * PAD] = head[:PAD]
    buf[h, 2 * PAD : PAD + rows] = head[PAD:] + tail[: rows - PAD]
    buf[h, PAD + rows : 2 * PAD + rows] = tail[rows - PAD :]
    buf[h, 2 * PAD + rows : 3 * PAD + rows] = zero


def conv(buf, h, taps, rows, first, sign):
    count = taps.shape[0]
    radius = count // 2
    span = rows + PAD
    total = jnp.zeros((span, LANES), F32)
    for k in range(count):
        total = total + taps[k : k + 1, lanes(h)] * buf[h, pl.ds(PAD + sign * (k - radius), span), :]
    return jnp.where(first, total[:rows], total[PAD:])


def tap_sums(out, values, buf, h, count, rows):
    radius = count // 2
    span = rows + PAD
    for k in range(count):
        prod = values * buf[h, pl.ds(PAD + k - radius, span), :]
        out[k : k + 1, lanes(h)] = jnp.sum(prod, axis=0, keepdims=True)


def fetches(sources, targets, sems):
    copies = [pltpu.make_async_copy(a, b, sems.at[i]) for i, (a, b) in enumerate(zip(sources, targets))]
    for copy in copies:
        copy.start()
    return copies


def batch_norm(conv_out, mean, inv_std, params, cols):
    norm = (conv_out[:, cols] - mean[:, cols]) * inv_std[:, cols]
    scaled = norm * params[0:1, cols] + params[1:2, cols]
    return norm, scaled, jax.nn.sigmoid(scaled)


def swish_slope(scaled, s):
    return s * (1.0 + scaled * (1.0 - s))


def gated(pre, live, h, channels):
    value = pre[:, lanes(h)]
    sig = jax.nn.sigmoid(pre[:, channels + h * LANES : channels + (h + 1) * LANES])
    return value, sig, jnp.where(live, value * sig, 0.0).astype(BF16).astype(F32)


def forward_kernel(
    len_ref, frames, proj, taps, raw_grad,
    conv_out, buf, pay, value_out, sig_out, given, pre, value, sig, spans, grad, sems,
):
    rows, channels = conv_out.shape
    first, live = own_masks(len_ref, rows)
    lane = lax.broadcasted_iota(jnp.int32, spans.shape, 1)
    spans[...] = jnp.where(
        lane == 0, len_ref[0, 0].astype(F32), jnp.where(lane == 1, len_ref[0, 1].astype(F32), 0.0)
    ).astype(BF16)
    (inward,) = fetches((raw_grad,), (grad,), sems)
    copies = fetches(
        (frames, spans), (given.at[pl.ds(0, rows)], given.at[pl.ds(2 * rows, 16)]), sems.at[pl.ds(1, 2)]
    )
    pre[...] = jnp.dot(frames[...], proj[...], preferred_element_type=F32)
    for h in range(channels // LANES):
        value[:, lanes(h)], sig[:, lanes(h)], glu = gated(pre, live, h, channels)
        embed(buf, h, glu, first)
    copies += fetches((value, sig), (value_out, sig_out), sems.at[pl.ds(3, 2)])
    sums = []
    for h in range(channels // LANES):
        out = jnp.where(live, conv(buf, h, taps, rows, first, 1), 0.0)
        conv_out[:, lanes(h)] = out
        sums.append(
            jnp.concatenate(
                [jnp.sum(out, axis=0, keepdims=True), jnp.sum(out * out, axis=0, keepdims=True)], axis=0
            )
        )
        if h == 0:
            inward.wait()
            copies += fetches((grad,), (given.at[pl.ds(rows, rows)],), sems.at[pl.ds(5, 1)])
    both = jnp.concatenate(sums, axis=1)
    pay[...] = jnp.broadcast_to(both[None], pay.shape)
    for copy in copies:
        copy.wait()


def live_taps(split, end, rows):
    dims = (TAPS + 1, rows + 3 * PAD)
    tap = lax.broadcasted_iota(jnp.int32, dims, 0)
    at = lax.broadcasted_iota(jnp.int32, dims, 1) - tap + TAPS // 2
    one = (at >= PAD) & (at < PAD + split)
    two = (at >= 2 * PAD + split) & (at < 2 * PAD + end)
    return jnp.where(one | two, 1.0, 0.0).astype(BF16)


def side_kernel(
    len_ref, grad_out, proj_out, conv_out, buf, gain, shift, counts,
    grad_hidden, ones_sum, conv_sum, params, hid, work,
):
    rows, channels = conv_out.shape
    first, live = own_masks(len_ref, rows)
    marks = live_taps(len_ref[0, 0], len_ref[0, 0] + len_ref[0, 1], rows)
    hid[...] = jnp.dot(grad_out[...], proj_out[...], preferred_element_type=F32)
    for h in range(channels // LANES):
        cols = lanes(h)
        grad_hidden[:, cols] = jnp.where(live, hid[:, cols], 0.0)
        ones_sum[:, cols] = jnp.dot(marks, buf[h].astype(BF16), preferred_element_type=F32)
        embed(work, h, conv_out[:, cols], first)
        tap_sums(conv_sum, work[h, pl.ds(PAD, rows + PAD), :], buf, h, TAPS, rows)
        conv_sum[TAPS : TAPS + 1, cols] = jnp.zeros((1, LANES), F32)
    total = jnp.sum(counts[...].astype(F32), axis=1, keepdims=True) * BLOCK
    params[0:1] = gain[...]
    params[1:2] = shift[...]
    params[2:3] = jnp.broadcast_to(total, (1, channels))
    params[3:] = jnp.zeros((5, channels), F32)


def mirror_kernel(
    given, proj, proj_out, taps, stats, params, left_a, left_b, hidden_a,
    value, sig, grad_hidden, conv_out, out_rows, ends, pre, hid, buf, hidden,
):
    rows, channels = conv_out.shape
    spans = given[2 * rows : 2 * rows + 16, :LANES].astype(F32)[0:1]
    split = spans[:, 0:1]
    end = split + spans[:, 1:2]
    ends[0:1] = jnp.broadcast_to(split, (1, LANES))
    ends[1:2] = jnp.broadcast_to(end, (1, LANES))
    ends[2:] = jnp.zeros((6, LANES), F32)
    first, live = row_masks(ends[0:1], ends[1:2], rows)
    mean, inv_std = stats[0:1], stats[1:2]
    pre[...] = jnp.dot(given[:rows], proj[...], preferred_element_type=F32)
    hid[...] = jnp.dot(given[rows : 2 * rows], proj_out[...], preferred_element_type=F32)
    for h in range(channels // LANES):
        cols = lanes(h)
        value[:, cols], sig[:, cols], glu = gated(pre, live, h, channels)
        embed(buf, h, glu, first)
        conv_out[:, cols] = jnp.where(live, conv(buf, h, taps, rows, first, 1), 0.0)
        grad_hidden[:, cols] = jnp.where(live, hid[:, cols], 0.0)
        _, scaled, s = batch_norm(conv_out, mean, inv_std, params, cols)
        hidden[:, cols] = jnp.where(live, scaled * s, 0.0).astype(BF16)
    total = jnp.dot(left_a[...], hidden_a[...], preferred_element_type=F32)
    total = total + jnp.dot(left_b[...], hidden[...], preferred_element_type=F32)
    out_rows[...] = total.astype(BF16)


def norm_kernel(
    len_ref, got, params, conv_out, grad_hidden, buf, ones_sum, conv_sum,
    hidden, stats, sums, work,
):
    rows, channels = conv_out.shape
    count = TAPS
    first, live = own_masks(len_ref, rows)
    total = params[2:3]
    found = tree_sum(got[...])
    mean = found[0:1] / total
    inv_std = lax.rsqrt(found[1:2] / total - mean * mean + 1e-05)
    stats[0:1] = mean
    stats[1:2] = inv_std
    base = 3 * (count + 1)
    sums[count + 1 : 2 * (count + 1)] = ones_sum[...]
    sums[2 * (count + 1) : base] = conv_sum[...]
    sums[base + 2 :] = jnp.zeros((6, channels), F32)
    for h in range(channels // LANES):
        cols = lanes(h)
        norm, scaled, s = batch_norm(conv_out, mean, inv_std, params, cols)
        hidden[:, cols] = jnp.where(live, scaled * s, 0.0).astype(BF16)
        grad = grad_hidden[:, cols] * swish_slope(scaled, s)
        sums[base : base + 1, cols] = jnp.sum(grad, axis=0, keepdims=True)
        sums[base + 1 : base + 2, cols] = jnp.sum(grad * norm, axis=0, keepdims=True)
        embed(work, h, grad, first)
        tap_sums(sums, work[h, pl.ds(PAD, rows + PAD), :], buf, h, count, rows)
        sums[count : count + 1, cols] = jnp.zeros((1, LANES), F32)


def spread_kernel(own, other, pay, sums):
    sums[...] = own[...] + other[...]
    count = pay.shape[0] // 2
    base = 3 * count
    tile = jnp.concatenate(
        [sums[base + i : base + i + 1, lanes(h)] for i in range(2) for h in range(2)]
        + [jnp.zeros((4, LANES), F32)],
        axis=0,
    )
    pay[...] = jnp.broadcast_to(tile[None], pay.shape)
    for j in range(pay.shape[0]):
        for i in range(3):
            at = i * count + j // 2
            pay[j, 4 + i : 5 + i, :] = sums[at : at + 1, lanes(j % 2)]


def back_kernel(
    len_ref, half_ref, ends, got, params, stats, conv_a, conv_b, taps,
    hid_a, hid_b, value_a, value_b, sig_a, sig_b, left_a, left_b, rows_in,
    own_pre, shift_grad, gain_grad, pay, work, grad_pre, hids, values, sigs, left, out_rows, sems,
):
    rows, channels = conv_a.shape
    width = 2 * channels
    peers, rows_dev, _ = pay.shape
    copies = fetches(
        (hid_a, hid_b, value_a, value_b, sig_a, sig_b, left_a, left_b, rows_in),
        (
            hids.at[0], hids.at[1], values.at[0], values.at[1], sigs.at[0], sigs.at[1],
            left.at[0], left.at[1], out_rows,
        ),
        sems,
    )
    total = params[2:3]
    sums = tree_sum(got[...])
    mean, inv_std = stats[0:1], stats[1:2]
    slices, scales, means = [], [], []
    for h in range(channels // LANES):
        cols = lanes(h)
        s, q = sums[h : h + 1], sums[2 + h : 3 + h]
        shift_grad[:, cols] = s
        gain_grad[:, cols] = q
        scale = params[0:1, cols] * inv_std[:, cols]
        s, q = s / total[:, cols], q / total[:, cols]
        own, ones, cv = sums[4:5], sums[5:6], sums[6:7]
        slices.append(scale * (own - s * ones - q * inv_std[:, cols] * (cv - mean[:, cols] * ones)))
        scales.append(scale)
        means.append((s, q))
    for part, conv_out in enumerate((conv_a, conv_b)):
        masks = own_masks(len_ref, rows) if part == 0 else row_masks(ends[0:1], ends[1:2], rows)
        first, live = masks
        span = slice(part * rows, (part + 1) * rows)
        for h in range(channels // LANES):
            cols = lanes(h)
            s, q = means[h]
            norm, scaled, swish = batch_norm(conv_out, mean, inv_std, params, cols)
            slope = swish_slope(scaled, swish)
            if h == 0:
                copies[part].wait()
            grad = scales[h] * (hids[part, :, cols] * slope - s - norm * q)
            embed(work, h, jnp.where(live, grad, 0.0), first)
            glu = jnp.where(live, conv(work, h, taps, rows, first, -1), 0.0)
            if h == 0:
                copies[2 + part].wait()
                copies[4 + part].wait()
            v, g = values[part, :, cols], sigs[part, :, cols]
            grad_pre[span, cols] = (glu * g).astype(BF16)
            grad_pre[span, channels + h * LANES : channels + (h + 1) * LANES] = (
                glu * v * g * (1.0 - g)
            ).astype(BF16)
        copies[6 + part].wait()
        term = jnp.dot(left[part], grad_pre[span], preferred_element_type=F32)
        total = term if part == 0 else total + term
    own_pre[...] = grad_pre[:rows]
    which = jnp.full((1, LANES), half_ref[0], jnp.int32)
    depth = jnp.where(which == 0, slices[0], slices[1]).astype(BF16)
    copies[8].wait()
    pay[:, :, :width] = total.reshape(peers, rows_dev, width).astype(BF16)
    pay[:, :, width : width + channels] = out_rows[...]
    pay[:, :, width + channels :] = jnp.broadcast_to(depth[None], (peers, rows_dev, LANES))


def frame_kernel(mp_ref, grad_pre, proj, own, one, two, three):
    width = own.shape[1]
    groups = proj.shape[0] // width
    for d, out in enumerate((own, one, two, three)):
        at = pl.multiple_of(lax.rem(mp_ref[0] + d, groups) * width, width)
        term = lax.dot_general(grad_pre[...], proj[pl.ds(at, width), :], NT, preferred_element_type=F32)
        out[...] = term.astype(BF16)


def last_kernel(got, in_rows, out_rows, depth):
    more = out_rows.shape[1]
    width = 2 * more
    for g in range(2):
        total = jnp.zeros((in_rows.shape[0], more), F32)
        for j in range(got.shape[0]):
            total = total + got[j, :, g * more : (g + 1) * more].astype(F32)
        in_rows[:, g, :] = total
    total = jnp.zeros((in_rows.shape[0], more), F32)
    for j in range(got.shape[0]):
        total = total + got[j, :, width : width + more].astype(F32)
    out_rows[...] = total
    for j in range(2 * depth.shape[0]):
        depth[j // 2 : j // 2 + 1, lanes(j % 2)] = got[j, 0:1, width + more :].astype(F32)


def core_rows(x, core):
    frames, width = x.shape
    rows = x.T.reshape(width // 16, 2, 8, frames)
    return lax.dynamic_index_in_dim(rows, core, 1, keepdims=False).reshape(width // 2, frames)


def swap_cores(x):
    return lax.ppermute(x, "core", [(0, 1), (1, 0)])


def after(x, y):
    return lax.optimization_barrier((x, y))[0]


def shards(frames, proj_in, taps, bn_gain, bn_shift, proj_out, grad_out, counts, lengths):
    rows, width = frames.shape
    channels = proj_in.shape[2]
    count = taps.shape[0]
    halves = channels // LANES
    buf_rows = rows + 3 * PAD
    peers = lax.axis_size(DP)
    chips = lax.axis_size(YZ)
    groups = lax.axis_size("mp")
    rows_dev = width // peers
    core = lax.axis_index("core")
    chip = lax.axis_index(YZ)
    mp = lax.axis_index("mp")
    full = shape((rows, channels))
    buf_shape = (halves, buf_rows, LANES)
    tap_shape = (count + 1, channels)
    wide = pltpu.VMEM((rows, 2 * channels), F32)
    square = pltpu.VMEM((rows, channels), F32)
    work = pltpu.VMEM(buf_shape, F32)
    proj = proj_in.reshape(width, 2 * channels)
    counts_row = counts.reshape(1, -1)
    gain_row = bn_gain.reshape(1, channels)
    shift_row = bn_shift.reshape(1, channels)

    conv_a, buf_a, pay, value_a, sig_a, given = call(
        forward_kernel,
        (
            full,
            shape(buf_shape),
            hbm_shape((peers, 2, channels)),
            hbm_shape((rows, channels)),
            hbm_shape((rows, channels)),
            hbm_shape((2 * rows + 16, width), BF16),
        ),
        [SM, VM, VM, VM, AN],
        [
            wide,
            square,
            square,
            pltpu.VMEM((16, width), BF16),
            pltpu.VMEM((rows, width), BF16),
            pltpu.SemaphoreType.DMA((6,)),
        ],
        out_specs=(VM, VM, VM, AN, AN, AN),
    )(lengths, frames, proj, taps, grad_out)
    got = lax.all_to_all(pay, DP, 0, 0)

    given = swap_cores(given)
    hid_a, ones_a, conv_sum_a, params = call(
        side_kernel,
        (
            full,
            shape(tap_shape),
            shape(tap_shape),
            shape((8, channels)),
        ),
        [SM, HB, HB, VM, VM, HB, HB, HB],
        [square, work],
    )(lengths, grad_out, proj_out, conv_a, buf_a, gain_row, shift_row, counts_row)
    late = lax.optimization_barrier((frames, grad_out, params))
    left_in_a = core_rows(late[0], core)
    left_out_a = core_rows(late[1], core)
    got, left_in_a, left_out_a = lax.optimization_barrier((got, left_in_a, left_out_a))

    hidden_a, stats, sums = call(
        norm_kernel,
        (
            shape((rows, channels), BF16),
            shape((2, channels)),
            shape((3 * (count + 1) + 8, channels)),
        ),
        [SM] + [VM] * 7,
        [work],
    )(lengths, got, params, conv_a, hid_a, buf_a, ones_a, conv_sum_a)
    (pay,) = call(
        spread_kernel,
        (hbm_shape((chips, 8, LANES)),),
        [VM, VM],
        [pltpu.VMEM((3 * (count + 1) + 8, channels), F32)],
    )(sums, swap_cores(sums))
    got = lax.all_to_all(pay, YZ, 0, 0)

    given = after(given, pay)
    left_in_b = core_rows(given[:rows], core)
    left_out_b = core_rows(given[rows : 2 * rows], core)
    value_b, sig_b, hid_b, conv_b, out_rows, ends = call(
        mirror_kernel,
        (
            hbm_shape((rows, channels)),
            hbm_shape((rows, channels)),
            hbm_shape((rows, channels)),
            full,
            hbm_shape((width // 2, channels), BF16),
            shape((8, LANES)),
        ),
        [HB, HB, HB, HB, VM, VM, HB, VM, VM],
        [wide, square, work, pltpu.VMEM((rows, channels), BF16)],
    )(given, proj, proj_out, taps, stats, params, left_out_a, left_out_b, hidden_a)
    got, out_rows, left_in_a, left_in_b = lax.optimization_barrier((got, out_rows, left_in_a, left_in_b))
    out_rows = out_rows.reshape(chips, rows_dev, channels)

    half = (chip % 2).astype(jnp.int32).reshape(1)
    grad_pre, shift_grad, gain_grad, pay = call(
        back_kernel,
        (
            shape((rows, 2 * channels), BF16),
            hbm_shape((1, channels)),
            hbm_shape((1, channels)),
            hbm_shape((chips, rows_dev, 3 * channels + LANES), BF16),
        ),
        [SM, SM] + [VM] * 7 + [AN] * 9,
        [
            work,
            pltpu.VMEM((2 * rows, 2 * channels), BF16),
            pltpu.VMEM((2, rows, channels), F32),
            pltpu.VMEM((2, rows, channels), F32),
            pltpu.VMEM((2, rows, channels), F32),
            pltpu.VMEM((2, width // 2, rows), BF16),
            pltpu.VMEM((chips, rows_dev, channels), BF16),
            pltpu.SemaphoreType.DMA((9,)),
        ],
    )(
        lengths, half, ends, got, params, stats, conv_a, conv_b, taps,
        hid_a, hid_b, value_a, value_b, sig_a, sig_b, left_in_a, left_in_b, out_rows,
    )
    got = lax.all_to_all(pay, YZ, 0, 0)

    term = shape((rows, width // groups), BF16)
    own, one, two, three = call(frame_kernel, (term,) * 4, [SM, VM, HB])(
        mp.astype(jnp.int32).reshape(1), grad_pre, proj
    )

    frame_sum = own.astype(F32)
    for d, part in ((1, one), (2, two), (3, three)):
        part = lax.ppermute(after(part, pay), "mp", [(i, (i + d) % groups) for i in range(groups)])
        frame_sum = frame_sum + part.astype(F32)
    frame_grad = frame_sum.astype(BF16)

    in_grad, out_grad, depth_grad = call(
        last_kernel,
        (hbm_shape((rows_dev, 2, channels)), hbm_shape((rows_dev, channels)), hbm_shape((count, channels))),
        [VM],
    )(got)
    return (frame_grad, in_grad, out_grad, depth_grad, gain_grad.reshape(channels), shift_grad.reshape(channels))


def solution(mesh):
    grid = Mesh(mesh.devices.reshape(8, 8, 2, 4), ("y", "z", "core", "mp"))
    placed = (
        P(DP, None),
        P(None, None, "mp"),
        P(None, "mp"),
        P("mp"),
        P("mp"),
        P(None, "mp"),
        P(DP, None),
        P(),
        P(DP, None),
    )
    return jax.shard_map(
        shards,
        mesh=grid,
        in_specs=placed,
        out_specs=(
            P(DP, "mp"),
            P(DP, None, "mp"),
            P(DP, "mp"),
            P(None, "mp"),
            P("mp"),
            P("mp"),
        ),
        check_vma=False,
    )
```
